128 devices in a mesh: blocks: 128 (over y, x, z, core).
Axes of the slice: x: 4, y: 4, z: 4, core: 2. Of those that a mesh axis runs over, the one named last changes fastest.
Arguments:
- old_pdfs: float32 [256, 19, 32768], P('blocks'), may hold values from 0 to 0.5
- old_slot: int32 [128], replicated, may hold values from 0 to 255, as said below
- neighbours: int32 [128, 18], P('blocks'), may hold values from -1 to 127, as said below
- cell_flags: int32 [128, 32768], P('blocks'), may hold values from 0 to 3, as said below
Outputs:
- new_pdfs: float32 [128, 19, 32768], P('blocks')
The draws below stay inside these ranges and needn't reach their ends.
Inputs may be any that keep to these rules, and one draw needn't show every extreme that they name: `old_slot`: distinct slots; slot s lies on device s // 2 before migration; in every draw some device has all 2 of its slots in use. `neighbours`: the blocks form 32 layers of 2 x 2 blocks along a vessel, blocks 4 * l to 4 * l + 3 making layer l; column d names the block at block offset c_(d+1), or -1 where there is none; the relation is mutual. `cell_flags`: 0 fluid, 1 wall, 2 inlet, 3 outlet; the cells on the outermost layer of every block are fluid.
All inputs are finite; a program needn't handle non-finite values.
Results may differ from the reference program's by a relative error of at most 0.0003.
Values sent between devices are 32-bit elements; how exact they have to be, the bound alone decides.
No kernel may reach another device: no remote copies, remote signals or barrier semaphores. Data moves between devices by JAX's collectives and lax.ppermute only.
A program may use at most 192 MiB of HBM per device.

```python
import jax
import jax.numpy as jnp
import numpy as np
from jax import lax

EDGE = 32
STEPS = 2
SLOT_DEV = 2
FLUID_BLOCKS = 128
ALL_SLOTS = 256
CELLS = 32768


VELOCITY = ((0, 0, 0), (1, 0, 0), (-1, 0, 0), (0, 1, 0), (0, -1, 0), (0, 0, 1), (0, 0, -1), (1, 1, 0), (-1, -1, 0), (1, -1, 0), (-1, 1, 0), (1, 0, 1), (-1, 0, -1), (1, 0, -1), (-1, 0, 1), (0, 1, 1), (0, -1, -1), (0, 1, -1), (0, -1, 1))


WEIGHT_LIST = (1.0 / 3.0,) + (1.0 / 18.0,) * 6 + (1.0 / 36.0,) * 12


def draw_old_pdfs(key, part):
    weights = jnp.asarray(WEIGHT_LIST, jnp.float32)[None, :, None]
    normal_noise = jax.random.normal(key, (ALL_SLOTS, 19, CELLS), jnp.float32)
    return weights * (1.0 + 0.2 * jnp.clip(normal_noise, -2.0, 2.0))


def draw_old_slot(key, part):
    choose_key, score_key, order_key = jax.random.split(key, 3)
    full_device = jax.random.randint(choose_key, (), 0, ALL_SLOTS // SLOT_DEV)
    slot_index = jnp.arange(ALL_SLOTS, dtype=jnp.int32)
    scores = jax.random.randint(score_key, (ALL_SLOTS,), 0, 2 ** 20) * ALL_SLOTS + slot_index
    ordering = jnp.argsort(scores)
    elsewhere_flag = (ordering // SLOT_DEV != full_device).astype(jnp.int32)
    ordering = ordering[jnp.argsort(elsewhere_flag, stable=True)]
    chosen = ordering[:FLUID_BLOCKS]
    return jax.random.permutation(order_key, chosen).astype(jnp.int32)


def draw_neighbours(key, part):
    layer_count = FLUID_BLOCKS // 4
    scores = jax.random.randint(key, (layer_count, 4), 0, 2 ** 20) * 4 + jnp.arange(4, dtype=jnp.int32)
    placement = jnp.argsort(scores, axis=1).astype(jnp.int32)
    inverse = jnp.argsort(placement, axis=1).astype(jnp.int32)
    layer_index = jnp.arange(FLUID_BLOCKS, dtype=jnp.int32) // 4
    block_spot = placement.reshape(-1)
    across_x = block_spot % 2
    across_y = block_spot // 2
    columns = []
    for direction in VELOCITY[1:]:
        target_x = across_x + direction[0]
        target_y = across_y + direction[1]
        target_layer = layer_index + direction[2]
        inside = (target_x >= 0) & (target_x <= 1) & (target_y >= 0) & (target_y <= 1) & (target_layer >= 0) & (target_layer < layer_count)
        clipped_layer = jnp.clip(target_layer, 0, layer_count - 1)
        target_spot = jnp.clip(target_x, 0, 1) + 2 * jnp.clip(target_y, 0, 1)
        target = 4 * clipped_layer + inverse[clipped_layer, target_spot]
        columns.append(jnp.where(inside, target, -1))
    return jnp.stack(columns, axis=1).astype(jnp.int32)


def draw_cell_flags(key, part):
    raw_draw = jax.random.randint(key, (FLUID_BLOCKS, CELLS), 0, 100)
    cell_kind = jnp.where(raw_draw < 76, 0, jnp.where(raw_draw < 90, 1, jnp.where(raw_draw < 95, 2, 3)))
    cell_index = jnp.arange(CELLS, dtype=jnp.int32)
    coord_x = cell_index // (EDGE * EDGE)
    coord_y = cell_index // EDGE % EDGE
    coord_z = cell_index % EDGE
    outer_cell = (coord_x == 0) | (coord_x == EDGE - 1) | (coord_y == 0) | (coord_y == EDGE - 1) | (coord_z == 0) | (coord_z == EDGE - 1)
    return jnp.where(outer_cell[None, :], 0, cell_kind).astype(jnp.int32)


def setup_inputs(seed: int = 0) -> dict:
    keys = jax.random.split(jax.random.key(seed), 5)
    old_pdfs = draw_old_pdfs(jax.random.fold_in(keys[4], 71), 0)
    old_slot = draw_old_slot(jax.random.fold_in(keys[4], 71), 0)
    neighbours = draw_neighbours(jax.random.fold_in(keys[4], 71), 0)
    cell_flags = draw_cell_flags(jax.random.fold_in(keys[4], 71), 0)
    return dict(old_pdfs=old_pdfs, old_slot=old_slot, neighbours=neighbours, cell_flags=cell_flags)


VELOCITY = ((0, 0, 0), (1, 0, 0), (-1, 0, 0), (0, 1, 0), (0, -1, 0), (0, 0, 1), (0, 0, -1), (1, 1, 0), (-1, -1, 0), (1, -1, 0), (-1, 1, 0), (1, 0, 1), (-1, 0, -1), (1, 0, -1), (-1, 0, 1), (0, 1, 1), (0, -1, -1), (0, 1, -1), (0, -1, 1))
WEIGHT_LIST = (1.0 / 3.0,) + (1.0 / 18.0,) * 6 + (1.0 / 36.0,) * 12
RELAXATION = (0.0, 0.0, 0.0, 0.0, 1.19, 1.4, 1.2, 1.2, 1.2, 1.6, 1.6, 1.6, 1.6, 1.6, 1.4, 1.4, 1.98, 1.98, 1.98)
INLET_SPEED = (0.0, 0.0, 0.05)

def collision_table():
    lattice = np.array(VELOCITY) * 1.0
    along_x, along_y, along_z = (lattice[:, 0], lattice[:, 1], lattice[:, 2])
    squared = along_x * along_x + along_y * along_y + along_z * along_z
    monomials = [np.ones(19), along_x, along_y, along_z, squared, squared * squared, squared * along_x, squared * along_y, squared * along_z, 3.0 * along_x * along_x - squared, along_y * along_y - along_z * along_z, along_x * along_y, along_y * along_z, along_x * along_z, squared * (3.0 * along_x * along_x - squared), squared * (along_y * along_y - along_z * along_z), (along_y * along_y - along_z * along_z) * along_x, (along_z * along_z - along_x * along_x) * along_y, (along_x * along_x - along_y * along_y) * along_z]
    orthonormal = []
    for vector in monomials:
        for earlier in orthonormal:
            vector = vector - np.dot(vector, earlier) * earlier
        orthonormal.append(vector / np.sqrt(np.dot(vector, vector)))
    stacked = np.stack(orthonormal)
    return stacked.T * np.array(RELAXATION) @ stacked

def opposite(index_value):
    if index_value == 0:
        return 0
    return index_value + 1 if index_value % 2 == 1 else index_value - 1

def ghost_region(offset, edge_size):
    return tuple((slice(0, 1) if component < 0 else slice(edge_size + 1, edge_size + 2) if component > 0 else slice(1, edge_size + 1) for component in offset))

def outer_layer(offset, edge_size):
    return tuple((slice(edge_size - 1, edge_size) if component > 0 else slice(0, 1) if component < 0 else slice(0, edge_size) for component in offset))

def collide(values, collision):
    lattice = jnp.asarray(VELOCITY, jnp.float32).T
    weights = jnp.asarray(WEIGHT_LIST, jnp.float32)[None, :, None]
    density = lax.optimization_barrier(jnp.sum(values, axis=1, keepdims=True))
    momentum = jnp.einsum('ki,bin->bkn', lattice, values, precision=lax.Precision.HIGHEST)
    projected = jnp.einsum('ki,bkn->bin', lattice, momentum, precision=lax.Precision.HIGHEST)
    speed_square = lax.optimization_barrier(jnp.sum(momentum * momentum, axis=1, keepdims=True))
    balance = weights * (density + 3.0 * projected + 4.5 * projected * projected - 1.5 * speed_square)
    return values - jnp.einsum('pq,bqn->bpn', collision, values - balance, precision=lax.Precision.HIGHEST)

def propagate(padded, source_flags, collided_cells, block_flags):
    edge_size = block_flags.shape[-1]
    momentum = []
    for axis_index in range(3):
        running_sum = jnp.zeros_like(collided_cells[:, 0])
        for index_value in range(19):
            component = VELOCITY[index_value][axis_index]
            if component != 0:
                running_sum = running_sum + component * collided_cells[:, index_value]
        momentum.append(running_sum)
    speed_square = momentum[0] * momentum[0] + momentum[1] * momentum[1] + momentum[2] * momentum[2]
    inlet_square = sum((component * component for component in INLET_SPEED))
    results = []
    for index_value in range(19):
        offset = VELOCITY[index_value]
        weight = WEIGHT_LIST[index_value]
        window_slice = tuple((slice(1 - component, 1 - component + edge_size) for component in offset))
        pulled = padded[(slice(None), index_value) + window_slice]
        source_kind = source_flags[(slice(None),) + window_slice]
        bounce = collided_cells[:, opposite(index_value)]
        inlet_along = sum((component * inlet_part for component, inlet_part in zip(offset, INLET_SPEED)))
        inlet_value = weight * (1.0 + 3.0 * inlet_along + 4.5 * inlet_along * inlet_along - 1.5 * inlet_square)
        outlet_along = offset[0] * momentum[0] + offset[1] * momentum[1] + offset[2] * momentum[2]
        outlet_value = weight * (1.0 + 3.0 * outlet_along + 4.5 * outlet_along * outlet_along - 1.5 * speed_square)
        new_value = jnp.where(source_kind == 0, pulled, jnp.where(source_kind == 1, bounce, jnp.where(source_kind == 2, inlet_value, outlet_value)))
        results.append(jnp.where(block_flags == 0, new_value, 0.0))
    return jnp.stack(results, axis=1)

def advance_block(collided_all, block_id, block_flags, neighbour_row):
    own_block = collided_all[block_id]
    padded = jnp.zeros((19, EDGE + 2, EDGE + 2, EDGE + 2), jnp.float32).at[:, 1:-1, 1:-1, 1:-1].set(own_block)
    source_flags = jnp.ones((EDGE + 2, EDGE + 2, EDGE + 2), jnp.int32).at[1:-1, 1:-1, 1:-1].set(block_flags)
    for direction_code in range(18):
        offset = VELOCITY[direction_code + 1]
        target = neighbour_row[direction_code]
        present = target >= 0
        other_block = collided_all[jnp.maximum(target, 0)]
        region = ghost_region(offset, EDGE)
        facing = outer_layer(tuple((-component for component in offset)), EDGE)
        padded = padded.at[(slice(None),) + region].set(other_block[(slice(None),) + facing])
        source_flags = source_flags.at[region].set(jnp.where(present, 0, 1).astype(jnp.int32))
    return propagate(padded[None], source_flags[None], own_block[None], block_flags[None])[0]

def reference(old_pdfs, old_slot, neighbours, cell_flags):
    collision = jnp.asarray(collision_table(), jnp.float32)
    pdf_state = jnp.take(old_pdfs, old_slot.astype(jnp.int32), axis=0)
    flags_all = cell_flags.reshape(FLUID_BLOCKS, EDGE, EDGE, EDGE)
    block_ids = jnp.arange(FLUID_BLOCKS, dtype=jnp.int32)
    for step_index in range(STEPS):
        collided = lax.map(lambda single_block: collide(single_block[None], collision)[0], pdf_state)
        collided_all = collided.reshape(FLUID_BLOCKS, 19, EDGE, EDGE, EDGE)

        def advance(entry_tuple):
            return advance_block(collided_all, entry_tuple[0], entry_tuple[1], entry_tuple[2])
        pdf_state = lax.map(advance, (block_ids, flags_all, neighbours)).reshape(FLUID_BLOCKS, 19, CELLS)
    return pdf_state
```

```python
import functools

import jax
import jax.numpy as jnp
from jax import lax
from jax.experimental import pallas as pl
from jax.experimental.pallas import tpu as pltpu
from jax.sharding import PartitionSpec as P

EDGE = 32
VELOCITY = (
    (0, 0, 0),
    (1, 0, 0),
    (-1, 0, 0),
    (0, 1, 0),
    (0, -1, 0),
    (0, 0, 1),
    (0, 0, -1),
    (1, 1, 0),
    (-1, -1, 0),
    (1, -1, 0),
    (-1, 1, 0),
    (1, 0, 1),
    (-1, 0, -1),
    (1, 0, -1),
    (-1, 0, 1),
    (0, 1, 1),
    (0, -1, -1),
    (0, 1, -1),
    (0, -1, 1),
)
WEIGHT = (1.0 / 3.0,) + (1.0 / 18.0,) * 6 + (1.0 / 36.0,) * 12
INLET = (0.0, 0.0, 0.05)
WALL = 1e30
OUTLET = 2e30

REST = [3, 4, 5, 6, 7, 8, 9, 10, 11, 12, 13, 14, 15, 16, 17, 18]
POSITION = dict(zip((7, 11, 15), (7, 11, 15)))
POSITION = {0: 7, 1: 11, 2: 15}
POSITION.update(
    zip(REST, [q for q in range(19) if q not in (7, 11, 15)])
)
FACE_PDFS = [
    [i for i in range(19) if VELOCITY[i][axis] == side]
    for axis in range(3)
    for side in (1, -1)
]
CARRIERS = [(0, 7), (1, 10), (2, 7), (3, 9), (4, 15), (5, 17)]
TABLE_LANE = 104


def opposite(i):
    return 0 if i == 0 else (i + 1 if i % 2 == 1 else i - 1)


def ghost_places():
    places = {}
    plain = [
        (f, i) for f in range(6) for i in FACE_PDFS[f] if (f, i) not in CARRIERS
    ]
    for n, item in enumerate(plain):
        places[item] = (120 + n // 3, 1 + n % 3)
    for n, item in enumerate(CARRIERS + ["EA", "EB"]):
        places[item] = (120 + n, 4)
    return places


GHOST = ghost_places()


def tile_at(i, x):
    pos = POSITION[i]
    chunk = (pos % 4) * 32 + x
    place = pos // 4
    if pos in (7, 11, 15):
        far = x >= 24
        if isinstance(x, int):
            if far:
                return 72 + 8 * ((pos - 7) // 4) + x, 4
            return chunk, place
        chunk = jnp.where(far, 72 + 8 * ((pos - 7) // 4) + x, chunk)
        place = jnp.where(far, 4, place)
    return chunk, place


def inlet_value(i):
    along = sum(c * v for c, v in zip(VELOCITY[i], INLET))
    square = sum(v * v for v in INLET)
    return WEIGHT[i] * (1.0 + 3.0 * along + 4.5 * along * along - 1.5 * square)


def iotas():
    row = lax.broadcasted_iota(jnp.int32, (8, 128), 0)
    lane = lax.broadcasted_iota(jnp.int32, (8, 128), 1)
    return row, lane


def momentum(f):
    jx = (f[1] - f[2]) + (f[7] - f[8]) + (f[9] - f[10]) + (f[11] - f[12]) + (f[13] - f[14])
    jy = (f[3] - f[4]) + (f[7] - f[8]) - (f[9] - f[10]) + (f[15] - f[16]) + (f[17] - f[18])
    jz = (f[5] - f[6]) + (f[11] - f[12]) - (f[13] - f[14]) + (f[15] - f[16]) - (f[17] - f[18])
    return jx, jy, jz


def collide(f):
    even = {i: f[i] + f[i + 1] for i in range(1, 19, 2)}
    odd = {i: f[i] - f[i + 1] for i in range(1, 19, 2)}
    x_xy, y_xy = odd[7] + odd[9], odd[7] - odd[9]
    x_xz, z_xz = odd[11] + odd[13], odd[11] - odd[13]
    y_yz, z_yz = odd[15] + odd[17], odd[15] - odd[17]
    edge_x, edge_y, edge_z = x_xy + x_xz, y_xy + y_yz, z_xz + z_yz
    jx, jy, jz = odd[1] + edge_x, odd[3] + edge_y, odd[5] + edge_z
    flux = [
        edge - 4.0 * axis + (2.0 / 3.0) * j
        for edge, axis, j in ((edge_x, odd[1], jx), (edge_y, odd[3], jy), (edge_z, odd[5], jz))
    ]
    third_x, third_y, third_z = x_xy - x_xz, y_xy - y_yz, z_xz - z_yz
    b_xy, b_xz, b_yz = even[7] + even[9], even[11] + even[13], even[15] + even[17]
    axes = even[1] + even[3] + even[5]
    edges = b_xy + b_xz + b_yz
    density = f[0] + axes + edges
    sx, sy, sz = jx * jx, jy * jy, jz * jz
    square = sx + sy + sz
    energy = -30.0 * f[0] - 11.0 * axes + 8.0 * edges + 11.0 * density - 19.0 * square
    fourth = 12.0 * f[0] - 4.0 * axes + edges - 3.0 * density + 5.5 * square
    rate_e, rate_f = 1.19 / 2394.0, 1.4 / 252.0
    out = [None] * 19
    out[0] = f[0] + (30.0 * rate_e) * energy - (12.0 * rate_f) * fourth
    axis_part = (11.0 * rate_e) * energy + (4.0 * rate_f) * fourth
    edge_part = (-8.0 * rate_e) * energy - rate_f * fourth
    axis_third, edge_third = axes * (1.0 / 3.0), edges * (1.0 / 3.0)
    third_square = square * (1.0 / 3.0)
    axis_delta, edge_delta = [], []
    for a, c, s in ((even[1], b_yz, sx), (even[3], b_xz, sy), (even[5], b_xy, sz)):
        alpha, gamma, tau = a - axis_third, c - edge_third, s - third_square
        p_mode = alpha - gamma - tau
        pi_mode = 0.5 * tau - 2.0 * alpha - gamma
        axis_delta.append(axis_part - (1.6 / 6.0) * p_mode + (2.8 / 12.0) * pi_mode)
        edge_delta.append(edge_part + (1.6 / 6.0) * p_mode + (1.4 / 12.0) * pi_mode)
    for k, i in enumerate((1, 3, 5)):
        odd_part = 0.12 * flux[k]
        out[i] = f[i] + (axis_delta[k] + odd_part)
        out[i + 1] = f[i + 1] + (axis_delta[k] - odd_part)
    fx, fy, fz = (0.03 * v for v in flux)
    hx, hy, hz = 0.2475 * third_x, 0.2475 * third_y, 0.2475 * third_z
    planes = (
        (7, 9, edge_delta[2], jx * jy, fx + hx, fy + hy),
        (11, 13, edge_delta[1], jx * jz, fx - hx, fz + hz),
        (15, 17, edge_delta[0], jy * jz, fy - hy, fz - hz),
    )
    for i, k, delta, cross, first, second in planes:
        shear = 0.4 * (even[i] - even[k] - cross)
        together, against = first + second, first - second
        same, mixed = delta - shear, delta + shear
        out[i] = f[i] + (same - together)
        out[i + 1] = f[i + 1] + (same + together)
        out[k] = f[k] + (mixed - against)
        out[k + 1] = f[k + 1] + (mixed + against)
    return out


def roll_lanes(v, shift):
    if isinstance(shift, int):
        shift = shift % 128
        return v if shift == 0 else pltpu.roll(v, shift, 1)
    return pltpu.roll(v, shift & 127, 1)


def pack_y_face(load_rows, i, face, lane):
    up = face == 2
    packed = None
    for q in range(4):
        rows = load_rows(i, q, 7 if up else 0)
        moved = roll_lanes(rows, 32 * q - 96 if up else 32 * q)
        packed = moved if packed is None else jnp.where(lane // 32 == q, moved, packed)
    return packed


def add_z_faces(c, x, faces_ref, lane):
    here = lane % 32 == x
    n = 0
    for face in (4, 5):
        for i in FACE_PDFS[face]:
            rows = pl.ds(8 * n, 8)
            moved = roll_lanes(c[i], x - (31 if face == 4 else 0) + 128)
            faces_ref[rows, :] = jnp.where(here, moved, faces_ref[rows, :])
            n += 1


def pack_edges(plane, y_face, lane, edge_rows_ref):
    tile = jnp.zeros((8, 128), jnp.float32)
    for i in range(11, 19):
        cx, cy, cz = VELOCITY[i]
        source = plane(i, 31 if cx > 0 else 0) if cx else y_face[i]
        moved = roll_lanes(source, i - 11 - (31 if cz > 0 else 0))
        tile = jnp.where(lane % 32 == i - 11, moved, tile)
    edge_rows_ref[...] = jnp.zeros((8, 128), jnp.float32)
    for i in range(7, 11):
        cx, cy, _ = VELOCITY[i]
        line = plane(i, 31 if cx > 0 else 0)
        line = roll_lanes(line, 32 if cy > 0 else 0)
        row = 7 if cy > 0 else 0
        edge_rows_ref[i - 7 : i - 6, :] = line[row : row + 1, :]
    return tile


def pack_kernel(pdf_ref, neighbours_ref, out_ref, turn_ref, z_ref, edge_ref, table_ref):
    slot = pl.program_id(0)
    group = pl.program_id(1)
    row, lane = iotas()

    def rows_of(i, x):
        chunk, place = tile_at(i, x)
        return chunk * 80 + slot * 40 + place * 8

    for part in range(4):
        base = 192 * part
        for ct in range(8):
            for rt in range(3):
                high = min(19, rt * 8 + 8)
                at = base + ct * 24 + rt * 8
                turn_ref[at : at + high - rt * 8, :] = pdf_ref[
                    0, rt * 8 : high, part * 1024 + ct * 128 : part * 1024 + ct * 128 + 128
                ]
        f = [turn_ref[pl.ds(base + i, 8, stride=24), :] for i in range(19)]
        c = collide(f)
        x = group * 4 + part
        for i in range(19):
            out_ref[pl.ds(pl.multiple_of(rows_of(i, x), 8), 8), :] = c[i]
        add_z_faces(c, x, z_ref, lane)

    @pl.when(group == 7)
    def _():
        table_ref[...] = jnp.zeros((8, 128), jnp.float32)
        table_ref[7:8, 0:18] = neighbours_ref[...].astype(jnp.float32)
        table = roll_lanes(table_ref[...], TABLE_LANE)
        free = (row == 7) & (lane >= TABLE_LANE) & (lane < TABLE_LANE + 18)

        def plane(i, x):
            return out_ref[pl.ds(pl.multiple_of(rows_of(i, x), 8), 8), :]

        def load_rows(i, q, r):
            return out_ref[pl.ds(rows_of(i, q) + r, 8, stride=320), :]

        def put(key, value):
            chunk, place = GHOST[key]
            if place == 4:
                value = jnp.where(free, table, value)
            at = pl.multiple_of(chunk * 80 + slot * 40 + place * 8, 8)
            out_ref[pl.ds(at, 8), :] = value

        for face in (0, 1):
            for i in FACE_PDFS[face]:
                put((face, i), plane(i, 31 if face == 0 else 0))
        y_face = {}
        for face in (2, 3):
            for i in FACE_PDFS[face]:
                y_face[i] = pack_y_face(load_rows, i, face, lane)
                put((face, i), y_face[i])
        n = 0
        for face in (4, 5):
            for i in FACE_PDFS[face]:
                put((face, i), z_ref[8 * n : 8 * n + 8, :])
                n += 1
        put("EA", pack_edges(plane, y_face, lane, edge_ref))
        put("EB", edge_ref[...])


def pick_kernel(old_slot_ref, table_ref, info_ref, spread_ref, out_ref):
    me = info_ref[0]
    row, lane = iotas()

    def tile(slot, place):
        return spread_ref[pl.ds(pl.multiple_of(slot * 40 + place * 8, 8), 8), :]

    def store(n, place, value):
        out_ref[pl.ds(pl.multiple_of(n * 40 + place * 8, 8), 8), :] = value

    def slot_of(n, direction):
        other = jnp.clip(table_ref[n * 18 + direction], 0, 127)
        return old_slot_ref[other]

    def own(n, carry):
        slot = old_slot_ref[n]
        for place in range(5):
            store(n, place, tile(slot, place))
        return carry

    lax.fori_loop(0, 128, own, 0, unroll=4)

    @pl.when(me >= 120)
    def _():
        def ghosts(n, carry):
            for place in range(1, 5):
                store(n, place, tile(slot_of(n, info_ref[place]), place))
            return carry

        lax.fori_loop(0, 128, ghosts, 0, unroll=4)

    @pl.when(me == 126)
    def _():
        def merge(n, carry):
            value = jnp.zeros((8, 128), jnp.float32)
            for i in range(11, 19):
                value = jnp.where(
                    lane % 32 == i - 11, tile(slot_of(n, opposite(i) - 1), 4), value
                )
            store(n, 4, value)
            return carry

        lax.fori_loop(0, 128, merge, 0)

    @pl.when(me == 127)
    def _():
        def merge(n, carry):
            value = jnp.zeros((8, 128), jnp.float32)
            for i in range(7, 11):
                value = jnp.where(row == i - 7, tile(slot_of(n, opposite(i) - 1), 4), value)
            store(n, 4, value)
            return carry

        lax.fori_loop(0, 128, merge, 0)


Y_PDFS = FACE_PDFS[2] + FACE_PDFS[3]
Z_PDFS = FACE_PDFS[4] + FACE_PDFS[5]
X_PDFS = FACE_PDFS[0] + FACE_PDFS[1]


def prepare_ghosts(face_tile, edge_tile, edge_rows, there, gx_ref, gy_ref, gz_ref, lane):
    for n, i in enumerate(X_PDFS):
        face = n // 5
        gx_ref[8 * n : 8 * n + 8, :] = jnp.where(there(face ^ 1), face_tile(face, i), WALL)
    for n, i in enumerate(Z_PDFS):
        face = 4 + n // 5
        value = jnp.where(there(face ^ 1), face_tile(face, i), WALL)
        cx = VELOCITY[i][0]
        if cx:
            beyond = -1 if cx > 0 else 32
            line = roll_lanes(edge_tile, beyond - (i - 11))
            line = jnp.where(there(opposite(i) - 1), line, WALL)
            value = jnp.where(lane % 32 == beyond % 32, line, value)
        gz_ref[8 * n : 8 * n + 8, :] = value
    for n, i in enumerate(Y_PDFS):
        face = 2 + n // 5
        cx, cy, cz = VELOCITY[i]
        value = jnp.where(there(face ^ 1), face_tile(face, i), WALL)
        if cz:
            target = 0 if cz > 0 else 31
            line = roll_lanes(edge_tile, target - (i - 11))
            line = jnp.where(there(opposite(i) - 1), line, WALL)
            value = jnp.where(lane % 32 == target, line, roll_lanes(value, cz))
        r = 0 if cy > 0 else 7
        for q in range(4):
            moved = roll_lanes(value, (0 if cy > 0 else 96) - 32 * q)
            gy_ref[pl.ds(272 * n + (q + 1) * 8 + r, 8, stride=32), :] = moved
        if cx:
            line = jnp.where(there(opposite(i) - 1), edge_rows, WALL)
            line = roll_lanes(line, 0 if cy > 0 else 96)
            at = 272 * n + (0 if cx > 0 else 33 * 8) + r
            gy_ref[at : at + 1, :] = line[i - 7 : i - 6, :]


def advance(x, plane, gx_ref, gy_ref, gz_ref, fluid, row, lane):
    own = [plane(i, x) for i in range(19)]
    u = momentum(own)
    base = 1.0 - 1.5 * (u[0] * u[0] + u[1] * u[1] + u[2] * u[2])
    new = [jnp.where(fluid, own[0], 0.0)] + [None] * 18
    low, high = lane < 32, lane >= 96
    first, last = low & (row == 0), high & (row == 7)
    z = lane % 32
    for i in range(1, 19):
        cx, cy, cz = VELOCITY[i]
        if cx:
            inside = plane(i, jnp.clip(x - cx, 0, 31))
            n = X_PDFS.index(i)
            border = jnp.full((8, 128), x, jnp.int32) == (0 if cx > 0 else 31)
            source = jnp.where(border, gx_ref[8 * n : 8 * n + 8, :], inside)
        else:
            source = own[i]
        if cz:
            target = 0 if cz > 0 else 31
            n = Z_PDFS.index(i)
            ghost = roll_lanes(gz_ref[8 * n : 8 * n + 8, :], target - (x - cx) + 128)
            source = jnp.where(z == target, ghost, roll_lanes(source, cz))
        if cy:
            n = Y_PDFS.index(i)
            ghost = gy_ref[pl.ds(pl.multiple_of(272 * n + (x - cx + 1) * 8, 8), 8), :]
            turned = roll_lanes(source, 32 * cy)
            carried = pltpu.roll(turned, cy % 8, 0)
            source = jnp.where(low if cy > 0 else high, carried, turned)
            source = jnp.where(first if cy > 0 else last, ghost, source)
        new[i] = source
    for i in range(1, 19, 2):
        cx, cy, cz = VELOCITY[i]
        along = None
        for c, v in zip((cx, cy, cz), u):
            if c:
                along = v * float(c) if along is None else (along + v if c > 0 else along - v)
        even = WEIGHT[i] * (base + 4.5 * along * along)
        odd = (3.0 * WEIGHT[i]) * along
        for k, outlet, bounce in ((i, even + odd, own[i + 1]), (i + 1, even - odd, own[i])):
            value = jnp.where(new[k] < 1.5e30, bounce, outlet)
            value = jnp.where(new[k] < 1e29, new[k], value)
            new[k] = jnp.where(fluid, value, 0.0)
    return new


def masked(c, flag):
    fluid, inlet = flag == 0, flag == 2
    sentinel = jnp.where(flag == 1, WALL, OUTLET)
    return [c[0]] + [
        jnp.where(fluid, c[i], jnp.where(inlet, inlet_value(i), sentinel)) for i in range(1, 19)
    ]


def tile_rows(i, x):
    return pl.ds(pl.multiple_of((i * 32 + x) * 8, 8), 8)


def first_step_kernel(
    info_ref, in_ref, flag_ref, out_ref, near_ref, far_ref, m_ref, gx_ref, gy_ref, gz_ref, z_ref, edge_ref
):
    me = info_ref[18]
    row, lane = iotas()

    def there(d):
        return jnp.full((8, 128), info_ref[d], jnp.int32) >= 0

    def arrived(key):
        chunk, place = GHOST[key]
        return in_ref[chunk * 40 + place * 8 : chunk * 40 + place * 8 + 8, :]

    def flags(x):
        return flag_ref[pl.ds(pl.multiple_of(x * 8, 8), 8), :]

    prepare_ghosts(
        lambda face, i: arrived((face, i)),
        arrived("EA"),
        arrived("EB"),
        there,
        gx_ref,
        gy_ref,
        gz_ref,
        lane,
    )

    def mask_plane(x, carry):
        loaded = []
        for i in range(19):
            chunk, place = tile_at(i, x)
            loaded.append(in_ref[pl.ds(pl.multiple_of(chunk * 40 + place * 8, 8), 8), :])
        for i, value in enumerate(masked(loaded, flags(x))):
            m_ref[tile_rows(i, x), :] = value
        return carry

    lax.fori_loop(0, 32, mask_plane, 0)

    def step(x, carry):
        flag = flags(x)
        new = advance(
            x, lambda i, at: m_ref[tile_rows(i, at), :], gx_ref, gy_ref, gz_ref, flag == 0, row, lane
        )
        c = masked(collide(new), flag)
        for i in range(19):
            out_ref[tile_rows(i, x), :] = c[i]
        add_z_faces(c, x, z_ref, lane)
        return carry

    lax.fori_loop(0, 32, step, 0)

    def plane(i, x):
        return out_ref[tile_rows(i, x), :]

    def load_rows(i, q, r):
        return out_ref[pl.ds((i * 32 + q) * 8 + r, 8, stride=32), :]

    y_face = {}
    for face in (2, 3):
        for i in FACE_PDFS[face]:
            y_face[i] = pack_y_face(load_rows, i, face, lane)
    edge_tile = pack_edges(plane, y_face, lane, edge_ref)
    edge_rows = edge_ref[...]
    for d in range(18):
        other = info_ref[d]
        cz = VELOCITY[d + 1][2]
        pair = (other >> 3) == (me >> 3)

        def send(ref, slot, d=d):
            def put(k, value):
                ref[pl.ds(pl.multiple_of(slot * 40 + k * 8, 8), 8), :] = value

            if d < 6:
                for k, i in enumerate(FACE_PDFS[d]):
                    if d < 2:
                        value = plane(i, 31 if d == 0 else 0)
                    elif d < 4:
                        value = y_face[i]
                    else:
                        n = Z_PDFS.index(i) if d == 4 else 5 + FACE_PDFS[5].index(i)
                        value = z_ref[8 * n : 8 * n + 8, :]
                    put(k, value)
            else:
                put(0, edge_tile)
                put(1, edge_rows)

        if cz == 0:

            @pl.when(other >= 0)
            def _():
                send(near_ref, other & 7)

        else:

            @pl.when((other >= 0) & pair)
            def _():
                send(near_ref, other & 7)

            @pl.when((other >= 0) & jnp.logical_not(pair))
            def _():
                send(far_ref, (other + 4) & 7)


def last_step_kernel(
    info_ref, in_ref, flag_ref, near_ref, far_ref, out_ref, gx_ref, gy_ref, gz_ref, turn_ref
):
    group = pl.program_id(0)
    me = info_ref[18]
    row, lane = iotas()

    def there(d):
        return jnp.full((8, 128), info_ref[d], jnp.int32) >= 0

    def arrived(d, k):
        other = jnp.maximum(info_ref[d], 0)
        at = pl.ds(pl.multiple_of((other & 7) * 40 + k * 8, 8), 8)
        value = near_ref[at, :]
        if VELOCITY[d + 1][2]:
            pair = jnp.full((8, 128), (other >> 3) ^ (me >> 3), jnp.int32) == 0
            at = pl.ds(pl.multiple_of(((other + 4) & 7) * 40 + k * 8, 8), 8)
            value = jnp.where(pair, value, far_ref[at, :])
        return value

    @pl.when(group == 0)
    def _():
        edge_tile = jnp.zeros((8, 128), jnp.float32)
        for i in range(11, 19):
            edge_tile = jnp.where(lane % 32 == i - 11, arrived(opposite(i) - 1, 0), edge_tile)
        edge_rows = jnp.zeros((8, 128), jnp.float32)
        for i in range(7, 11):
            edge_rows = jnp.where(row == i - 7, arrived(opposite(i) - 1, 1), edge_rows)
        prepare_ghosts(
            lambda face, i: arrived(face ^ 1, FACE_PDFS[face].index(i)),
            edge_tile,
            edge_rows,
            there,
            gx_ref,
            gy_ref,
            gz_ref,
            lane,
        )

    for part in range(4):
        x = group * 4 + part
        fluid = flag_ref[pl.ds(pl.multiple_of(x * 8, 8), 8), :] == 0
        new = advance(
            x, lambda i, at: in_ref[tile_rows(i, at), :], gx_ref, gy_ref, gz_ref, fluid, row, lane
        )
        base = 192 * part
        for i in range(19):
            turn_ref[base + 8 * i : base + 8 * i + 8, :] = new[i]
        for rt in range(3):
            high = min(19, rt * 8 + 8)
            for ct in range(8):
                value = turn_ref[pl.ds(base + rt * 64 + ct, 8, stride=8), :]
                at = part * 1024 + ct * 128
                out_ref[0, rt * 8 : high, at : at + 128] = value[: high - rt * 8, :]


VMEM_LIMIT = 56 * 1024 * 1024
F32 = jnp.float32


def whole(shape):
    zeros = (0,) * len(shape)
    return pl.BlockSpec(shape, lambda *_: zeros)


def scratch(rows):
    return pltpu.VMEM((rows, 128), F32)


def per_device(old_pdfs, old_slot, neighbours, cell_flags):
    me = lax.axis_index("blocks").astype(jnp.int32)
    flags = cell_flags.reshape(256, 128)
    params = functools.partial(pltpu.CompilerParams, vmem_limit_bytes=VMEM_LIMIT)

    packed = pl.pallas_call(
        pack_kernel,
        grid=(2, 8),
        in_specs=[
            pl.BlockSpec((1, 19, 4096), lambda s, g: (s, 0, g)),
            pl.BlockSpec((1, 18), lambda s, g: (0, 0)),
        ],
        out_specs=whole((10240, 128)),
        out_shape=jax.ShapeDtypeStruct((10240, 128), F32),
        scratch_shapes=[scratch(768), scratch(80), scratch(8), scratch(8)],
        compiler_params=params(),
        name="pack",
    )(old_pdfs, neighbours)
    spread = lax.all_to_all(
        packed.reshape(128, 80, 128), "blocks", split_axis=0, concat_axis=0, tiled=True
    )

    table = spread[:, 39, TABLE_LANE : TABLE_LANE + 18].astype(jnp.int32).reshape(128 * 18)
    codes = []
    for chunk in range(120, 128):
        by_place = {GHOST[key][1]: key for key in GHOST if GHOST[key][0] == chunk}
        codes.append(
            [0] + [0 if isinstance(by_place[p], str) else by_place[p][0] ^ 1 for p in range(1, 5)]
        )
    code = jnp.asarray(codes, jnp.int32)[jnp.clip(me - 120, 0, 7)]
    info = jnp.where(jnp.arange(5) == 0, me, code).astype(jnp.int32)
    smem = pl.BlockSpec(memory_space=pltpu.SMEM)
    picked = pl.pallas_call(
        pick_kernel,
        in_specs=[smem, smem, smem, pl.BlockSpec(memory_space=pltpu.VMEM)],
        out_specs=pl.BlockSpec(memory_space=pltpu.VMEM),
        out_shape=jax.ShapeDtypeStruct((5120, 128), F32),
        compiler_params=params(),
        name="pick",
    )(old_slot, table, info, spread.reshape(10240, 128))
    arrived = lax.all_to_all(
        picked.reshape(128, 40, 128), "blocks", split_axis=0, concat_axis=0, tiled=True
    )

    own_info = jnp.concatenate([neighbours.reshape(18), me.reshape(1)])
    ghost_scratch = [scratch(80), scratch(2720), scratch(80)]
    vmem = pl.BlockSpec(memory_space=pltpu.VMEM)
    state, near, far = pl.pallas_call(
        first_step_kernel,
        in_specs=[smem, vmem, vmem],
        out_specs=[vmem] * 3,
        out_shape=[
            jax.ShapeDtypeStruct((4864, 128), F32),
            jax.ShapeDtypeStruct((320, 128), F32),
            jax.ShapeDtypeStruct((320, 128), F32),
        ],
        scratch_shapes=[scratch(4864)] + ghost_scratch + [scratch(80), scratch(8)],
        compiler_params=params(),
        name="first_step",
    )(own_info, arrived.reshape(5120, 128), flags)

    near_groups = [[8 * k + i for i in range(8)] for k in range(16)]
    far_groups = [[(8 * k + 4 + i) % 128 for i in range(8)] for k in range(16)]
    received = [
        lax.all_to_all(
            part.reshape(8, 40, 128),
            "blocks",
            split_axis=0,
            concat_axis=0,
            axis_index_groups=groups,
            tiled=True,
        ).reshape(320, 128)
        for part, groups in ((near, near_groups), (far, far_groups))
    ]

    return pl.pallas_call(
        last_step_kernel,
        grid=(8,),
        in_specs=[
            pl.BlockSpec(memory_space=pltpu.SMEM),
            whole((4864, 128)),
            whole((256, 128)),
            whole((320, 128)),
            whole((320, 128)),
        ],
        out_specs=pl.BlockSpec((1, 19, 4096), lambda g: (0, 0, g)),
        out_shape=jax.ShapeDtypeStruct((1, 19, 32768), F32),
        scratch_shapes=ghost_scratch + [scratch(768)],
        compiler_params=params(),
        name="last_step",
    )(own_info, state, flags, received[0], received[1])


def solution(mesh):
    in_specs = (P("blocks", None, None), P(), P("blocks", None), P("blocks", None))
    return jax.shard_map(
        per_device,
        mesh=mesh,
        in_specs=in_specs,
        out_specs=P("blocks", None, None),
        check_vma=False,
    )
```

```python
import jax
import jax.numpy as jnp
from jax import lax
from jax.experimental import pallas as pl
from jax.experimental.pallas import tpu as pltpu
from jax.sharding import PartitionSpec as P

EDGE = 32
VELOCITY = (
    (0, 0, 0),
    (1, 0, 0),
    (-1, 0, 0),
    (0, 1, 0),
    (0, -1, 0),
    (0, 0, 1),
    (0, 0, -1),
    (1, 1, 0),
    (-1, -1, 0),
    (1, -1, 0),
    (-1, 1, 0),
    (1, 0, 1),
    (-1, 0, -1),
    (1, 0, -1),
    (-1, 0, 1),
    (0, 1, 1),
    (0, -1, -1),
    (0, 1, -1),
    (0, -1, 1),
)
WEIGHT = (1.0 / 3.0,) + (1.0 / 18.0,) * 6 + (1.0 / 36.0,) * 12
INLET = (0.0, 0.0, 0.05)
WALL = 1e30
OUTLET = 2e30

REST = [3, 4, 5, 6, 7, 8, 9, 10, 11, 12, 13, 14, 15, 16, 17, 18]
POSITION = {0: 7, 1: 11, 2: 15}
POSITION.update(
    zip(REST, [q for q in range(19) if q not in (7, 11, 15)])
)
FACE_PDFS = [
    [i for i in range(19) if VELOCITY[i][axis] == side]
    for axis in range(3)
    for side in (1, -1)
]
Y_PDFS = FACE_PDFS[2] + FACE_PDFS[3]
Z_PDFS = FACE_PDFS[4] + FACE_PDFS[5]
X_PDFS = FACE_PDFS[0] + FACE_PDFS[1]
CARRIERS = [(0, 7), (1, 10), (2, 7), (3, 9), (4, 15), (5, 17)]
TABLE_LANE = 104


def opposite(i):
    return 0 if i == 0 else (i + 1 if i % 2 == 1 else i - 1)


def ghost_places():
    places = {}
    plain = [
        (f, i) for f in range(6) for i in FACE_PDFS[f] if (f, i) not in CARRIERS
    ]
    for n, item in enumerate(plain):
        places[item] = (120 + n // 3, 1 + n % 3)
    for n, item in enumerate(CARRIERS + ["EA", "EB"]):
        places[item] = (120 + n, 4)
    return places


GHOST = ghost_places()


def tile_at(i, x):
    pos = POSITION[i]
    chunk = (pos % 4) * 32 + x
    place = pos // 4
    if pos in (7, 11, 15):
        far = x >= 24
        if isinstance(x, int):
            if far:
                return 72 + 8 * ((pos - 7) // 4) + x, 4
            return chunk, place
        chunk = jnp.where(far, 72 + 8 * ((pos - 7) // 4) + x, chunk)
        place = jnp.where(far, 4, place)
    return chunk, place


def inlet_value(i):
    along = sum(c * v for c, v in zip(VELOCITY[i], INLET))
    square = sum(v * v for v in INLET)
    return WEIGHT[i] * (1.0 + 3.0 * along + 4.5 * along * along - 1.5 * square)


def iotas():
    row = lax.broadcasted_iota(jnp.int32, (8, 128), 0)
    lane = lax.broadcasted_iota(jnp.int32, (8, 128), 1)
    return row, lane


def momentum(f):
    jx = (f[1] - f[2]) + (f[7] - f[8]) + (f[9] - f[10]) + (f[11] - f[12]) + (f[13] - f[14])
    jy = (f[3] - f[4]) + (f[7] - f[8]) - (f[9] - f[10]) + (f[15] - f[16]) + (f[17] - f[18])
    jz = (f[5] - f[6]) + (f[11] - f[12]) - (f[13] - f[14]) + (f[15] - f[16]) - (f[17] - f[18])
    return jx, jy, jz


def collide(f):
    even = {i: f[i] + f[i + 1] for i in range(1, 19, 2)}
    odd = {i: f[i] - f[i + 1] for i in range(1, 19, 2)}
    x_xy, y_xy = odd[7] + odd[9], odd[7] - odd[9]
    x_xz, z_xz = odd[11] + odd[13], odd[11] - odd[13]
    y_yz, z_yz = odd[15] + odd[17], odd[15] - odd[17]
    edge_x, edge_y, edge_z = x_xy + x_xz, y_xy + y_yz, z_xz + z_yz
    jx, jy, jz = odd[1] + edge_x, odd[3] + edge_y, odd[5] + edge_z
    flux = [
        edge - 4.0 * axis + (2.0 / 3.0) * j
        for edge, axis, j in ((edge_x, odd[1], jx), (edge_y, odd[3], jy), (edge_z, odd[5], jz))
    ]
    third_x, third_y, third_z = x_xy - x_xz, y_xy - y_yz, z_xz - z_yz
    b_xy, b_xz, b_yz = even[7] + even[9], even[11] + even[13], even[15] + even[17]
    axes = even[1] + even[3] + even[5]
    edges = b_xy + b_xz + b_yz
    density = f[0] + axes + edges
    sx, sy, sz = jx * jx, jy * jy, jz * jz
    square = sx + sy + sz
    energy = -30.0 * f[0] - 11.0 * axes + 8.0 * edges + 11.0 * density - 19.0 * square
    fourth = 12.0 * f[0] - 4.0 * axes + edges - 3.0 * density + 5.5 * square
    rate_e, rate_f = 1.19 / 2394.0, 1.4 / 252.0
    out = [None] * 19
    out[0] = f[0] + (30.0 * rate_e) * energy - (12.0 * rate_f) * fourth
    axis_part = (11.0 * rate_e) * energy + (4.0 * rate_f) * fourth
    edge_part = (-8.0 * rate_e) * energy - rate_f * fourth
    axis_third, edge_third = axes * (1.0 / 3.0), edges * (1.0 / 3.0)
    third_square = square * (1.0 / 3.0)
    axis_delta, edge_delta = [], []
    for a, c, s in ((even[1], b_yz, sx), (even[3], b_xz, sy), (even[5], b_xy, sz)):
        alpha, gamma, tau = a - axis_third, c - edge_third, s - third_square
        p_mode = alpha - gamma - tau
        pi_mode = 0.5 * tau - 2.0 * alpha - gamma
        axis_delta.append(axis_part - (1.6 / 6.0) * p_mode + (2.8 / 12.0) * pi_mode)
        edge_delta.append(edge_part + (1.6 / 6.0) * p_mode + (1.4 / 12.0) * pi_mode)
    for k, i in enumerate((1, 3, 5)):
        odd_part = 0.12 * flux[k]
        out[i] = f[i] + (axis_delta[k] + odd_part)
        out[i + 1] = f[i + 1] + (axis_delta[k] - odd_part)
    fx, fy, fz = (0.03 * v for v in flux)
    hx, hy, hz = 0.2475 * third_x, 0.2475 * third_y, 0.2475 * third_z
    planes = (
        (7, 9, edge_delta[2], jx * jy, fx + hx, fy + hy),
        (11, 13, edge_delta[1], jx * jz, fx - hx, fz + hz),
        (15, 17, edge_delta[0], jy * jz, fy - hy, fz - hz),
    )
    for i, k, delta, cross, first, second in planes:
        shear = 0.4 * (even[i] - even[k] - cross)
        together, against = first + second, first - second
        same, mixed = delta - shear, delta + shear
        out[i] = f[i] + (same - together)
        out[i + 1] = f[i + 1] + (same + together)
        out[k] = f[k] + (mixed - against)
        out[k + 1] = f[k + 1] + (mixed + against)
    return out


def roll_lanes(v, shift):
    if isinstance(shift, int):
        shift = shift % 128
        return v if shift == 0 else pltpu.roll(v, shift, 1)
    return pltpu.roll(v, shift & 127, 1)


def pack_y_face(load_rows, i, face, lane):
    up = face == 2
    packed = None
    for q in range(4):
        rows = load_rows(i, q, 7 if up else 0)
        moved = roll_lanes(rows, 32 * q - 96 if up else 32 * q)
        packed = moved if packed is None else jnp.where(lane // 32 == q, moved, packed)
    return packed


def join_z_faces(c, x, faces, lane):
    here = lane % 32 == x
    for n, i in enumerate(Z_PDFS):
        moved = roll_lanes(c[i], x - (31 if n < 5 else 0) + 128)
        faces[n] = jnp.where(here, moved, faces[n]) if n in faces else moved


def store_z_faces(faces, group, z_ref, base, lane):
    here = lane % 32 // 4 == group
    for n in range(10):
        rows = slice(base + 8 * n, base + 8 * n + 8)
        z_ref[rows, :] = jnp.where(here, faces[n], z_ref[rows, :])


def pack_edges(plane, y_face, lane, edge_rows_ref):
    tile = jnp.zeros((8, 128), jnp.float32)
    for i in range(11, 19):
        cx, cy, cz = VELOCITY[i]
        source = plane(i, 31 if cx > 0 else 0) if cx else y_face[i]
        moved = roll_lanes(source, i - 11 - (31 if cz > 0 else 0))
        tile = jnp.where(lane % 32 == i - 11, moved, tile)
    edge_rows_ref[...] = jnp.zeros((8, 128), jnp.float32)
    for i in range(7, 11):
        cx, cy, _ = VELOCITY[i]
        line = plane(i, 31 if cx > 0 else 0)
        line = roll_lanes(line, 32 if cy > 0 else 0)
        row = 7 if cy > 0 else 0
        edge_rows_ref[i - 7 : i - 6, :] = line[row : row + 1, :]
    return tile


def pack_kernel(
    old_slot_ref, neighbours_ref, pdf_ref, out_ref, tiles_ref, z_ref, edge_ref, sem_ref
):
    group = pl.program_id(0)
    row, lane = iotas()

    def rows_of(i, x, slot):
        chunk, place = tile_at(i, x)
        return chunk * 80 + slot * 40 + place * 8

    for slot in range(2):
        faces = {}
        for part in range(4):
            f = [pdf_ref[i, pl.ds(part * 16 + slot, 8, stride=2), :] for i in range(19)]
            c = collide(f)
            x = group * 4 + part
            for i in range(19):
                tiles_ref[pl.ds(pl.multiple_of(rows_of(i, x, slot), 8), 8), :] = c[i]
            join_z_faces(c, x, faces, lane)
        store_z_faces(faces, group, z_ref, 80 * slot, lane)

    def send(m, first, count, sem):
        rows = pl.ds(pl.multiple_of((m * 32 + first) * 80, 8), count * 80)
        return pltpu.make_async_copy(tiles_ref.at[rows], out_ref.at[rows], sem_ref.at[sem])

    for m in range(3):
        send(m, group * 4, 4, m * 8 + group).start()

    @pl.when(group == 7)
    def _():
        table = jnp.zeros((8, 128), jnp.int32)
        for d in range(18):
            other = jnp.clip(neighbours_ref[0, d], 0, 127)
            table = jnp.where(lane == TABLE_LANE + d, old_slot_ref[other], table)
        table = table.astype(jnp.float32)
        free = (row == 7) & (lane >= TABLE_LANE) & (lane < TABLE_LANE + 18)

        def ghosts(slot, carry):
            def plane(i, x):
                return tiles_ref[pl.ds(pl.multiple_of(rows_of(i, x, slot), 8), 8), :]

            def load_rows(i, q, r):
                return tiles_ref[pl.ds(rows_of(i, q, slot) + r, 8, stride=320), :]

            def put(key, value):
                chunk, place = GHOST[key]
                if place == 4:
                    value = jnp.where(free, table, value)
                at = pl.multiple_of(chunk * 80 + slot * 40 + place * 8, 8)
                tiles_ref[pl.ds(at, 8), :] = value

            for face in (0, 1):
                for i in FACE_PDFS[face]:
                    put((face, i), plane(i, 31 if face == 0 else 0))
            y_face = {}
            for face in (2, 3):
                for i in FACE_PDFS[face]:
                    y_face[i] = pack_y_face(load_rows, i, face, lane)
                    put((face, i), y_face[i])
            for n, i in enumerate(Z_PDFS):
                face = 4 + n // 5
                put((face, i), z_ref[pl.ds(pl.multiple_of(80 * slot + 8 * n, 8), 8), :])
            put("EA", pack_edges(plane, y_face, lane, edge_ref))
            put("EB", edge_ref[...])
            return carry

        lax.fori_loop(0, 2, ghosts, 0)
        last = send(3, 0, 32, 24)
        last.start()
        for m in range(3):
            for g in range(8):
                send(m, g * 4, 4, m * 8 + g).wait()
        last.wait()


def ghost_code(me, place):
    code = jnp.int32(0)
    for key, (chunk, at) in GHOST.items():
        if at == place and not isinstance(key, str):
            code = jnp.where(me == chunk, key[0] ^ 1, code)
    return code


def pick_kernel(old_slot_ref, spread_ref, out_ref, table_ref, slots_ref, sem_ref):
    me = lax.axis_index("blocks")
    row, lane = iotas()

    def tile(slot, place):
        return spread_ref[pl.ds(pl.multiple_of(slot * 40 + place * 8, 8), 8), :]

    def store(n, place, value):
        out_ref[pl.ds(pl.multiple_of(n * 40 + place * 8, 8), 8), :] = value

    @pl.when(me < 120)
    def _():
        def own(n, carry):
            slot = old_slot_ref[n]
            for place in range(5):
                store(n, place, tile(slot, place))
            return carry

        lax.fori_loop(0, 128, own, 0, unroll=8)

    @pl.when(me >= 120)
    def _():
        for b in range(16):
            rows = spread_ref[pl.ds(b * 640 + 39, 8, stride=80), :]
            table_ref[8 * b : 8 * b + 8, :] = rows.astype(jnp.int32)
        copy = pltpu.make_async_copy(table_ref, slots_ref, sem_ref)
        copy.start()

        def own(n, carry):
            store(n, 0, tile(old_slot_ref[n], 0))
            return carry

        lax.fori_loop(0, 128, own, 0, unroll=8)
        copy.wait()

        def slot_of(n, direction):
            return slots_ref[n, TABLE_LANE + direction]

        codes = [ghost_code(me, place) for place in range(5)]

        def ghosts(n, carry):
            for place in range(1, 4):
                store(n, place, tile(slot_of(n, codes[place]), place))
            return carry

        lax.fori_loop(0, 128, ghosts, 0, unroll=8)

        @pl.when(me < 126)
        def _():
            def fourth(n, carry):
                store(n, 4, tile(slot_of(n, codes[4]), 4))
                return carry

            lax.fori_loop(0, 128, fourth, 0, unroll=8)

        @pl.when(me == 126)
        def _():
            def merge(n, carry):
                value = jnp.zeros((8, 128), jnp.float32)
                for i in range(11, 19):
                    value = jnp.where(
                        lane % 32 == i - 11, tile(slot_of(n, opposite(i) - 1), 4), value
                    )
                store(n, 4, value)
                return carry

            lax.fori_loop(0, 128, merge, 0, unroll=2)

        @pl.when(me == 127)
        def _():
            def merge(n, carry):
                value = jnp.zeros((8, 128), jnp.float32)
                for i in range(7, 11):
                    value = jnp.where(row == i - 7, tile(slot_of(n, opposite(i) - 1), 4), value)
                store(n, 4, value)
                return carry

            lax.fori_loop(0, 128, merge, 0, unroll=2)


def prepare_ghosts(face_tile, edge_tile, edge_rows, there, gx_ref, gy_ref, gz_ref, lane):
    for n, i in enumerate(X_PDFS):
        face = n // 5
        gx_ref[8 * n : 8 * n + 8, :] = jnp.where(there(face ^ 1), face_tile(face, i), WALL)
    for n, i in enumerate(Z_PDFS):
        face = 4 + n // 5
        value = jnp.where(there(face ^ 1), face_tile(face, i), WALL)
        cx = VELOCITY[i][0]
        if cx:
            beyond = -1 if cx > 0 else 32
            line = roll_lanes(edge_tile, beyond - (i - 11))
            line = jnp.where(there(opposite(i) - 1), line, WALL)
            value = jnp.where(lane % 32 == beyond % 32, line, value)
        gz_ref[8 * n : 8 * n + 8, :] = value
    for n, i in enumerate(Y_PDFS):
        face = 2 + n // 5
        cx, cy, cz = VELOCITY[i]
        value = jnp.where(there(face ^ 1), face_tile(face, i), WALL)
        if cz:
            target = 0 if cz > 0 else 31
            line = roll_lanes(edge_tile, target - (i - 11))
            line = jnp.where(there(opposite(i) - 1), line, WALL)
            value = jnp.where(lane % 32 == target, line, roll_lanes(value, cz))
        r = 0 if cy > 0 else 7
        for q in range(4):
            moved = roll_lanes(value, (0 if cy > 0 else 96) - 32 * q)
            gy_ref[pl.ds(272 * n + (q + 1) * 8 + r, 8, stride=32), :] = moved
        if cx:
            line = jnp.where(there(opposite(i) - 1), edge_rows, WALL)
            line = roll_lanes(line, 0 if cy > 0 else 96)
            at = 272 * n + (0 if cx > 0 else 33 * 8) + r
            gy_ref[at : at + 1, :] = line[i - 7 : i - 6, :]


def advance(x, plane, gx_ref, gy_ref, gz_ref, fluid, row, lane):
    own = [plane(i, x) for i in range(19)]
    u = momentum(own)
    base = 1.0 - 1.5 * (u[0] * u[0] + u[1] * u[1] + u[2] * u[2])
    new = [jnp.where(fluid, own[0], 0.0)] + [None] * 18
    low, high = lane < 32, lane >= 96
    first, last = low & (row == 0), high & (row == 7)
    z = lane % 32
    for i in range(1, 19):
        cx, cy, cz = VELOCITY[i]
        if cx:
            inside = plane(i, jnp.clip(x - cx, 0, 31))
            n = X_PDFS.index(i)
            border = jnp.full((8, 128), x, jnp.int32) == (0 if cx > 0 else 31)
            source = jnp.where(border, gx_ref[8 * n : 8 * n + 8, :], inside)
        else:
            source = own[i]
        if cz:
            target = 0 if cz > 0 else 31
            n = Z_PDFS.index(i)
            ghost = roll_lanes(gz_ref[8 * n : 8 * n + 8, :], target - (x - cx) + 128)
            source = jnp.where(z == target, ghost, roll_lanes(source, cz))
        if cy:
            n = Y_PDFS.index(i)
            ghost = gy_ref[pl.ds(pl.multiple_of(272 * n + (x - cx + 1) * 8, 8), 8), :]
            turned = roll_lanes(source, 32 * cy)
            carried = pltpu.roll(turned, cy % 8, 0)
            source = jnp.where(low if cy > 0 else high, carried, turned)
            source = jnp.where(first if cy > 0 else last, ghost, source)
        new[i] = source
    for i in range(1, 19, 2):
        cx, cy, cz = VELOCITY[i]
        along = None
        for c, v in zip((cx, cy, cz), u):
            if c:
                along = v * float(c) if along is None else (along + v if c > 0 else along - v)
        even = WEIGHT[i] * (base + 4.5 * along * along)
        odd = (3.0 * WEIGHT[i]) * along
        for k, outlet, bounce in ((i, even + odd, own[i + 1]), (i + 1, even - odd, own[i])):
            value = jnp.where(new[k] < 1.5e30, bounce, outlet)
            value = jnp.where(new[k] < 1e29, new[k], value)
            new[k] = jnp.where(fluid, value, 0.0)
    return new


def masked(c, flag):
    fluid, inlet = flag == 0, flag == 2
    sentinel = jnp.where(flag == 1, WALL, OUTLET)
    return [c[0]] + [
        jnp.where(fluid, c[i], jnp.where(inlet, inlet_value(i), sentinel)) for i in range(1, 19)
    ]


def tile_rows(i, x):
    return pl.ds(pl.multiple_of((i * 32 + x) * 8, 8), 8)


def first_step_kernel(
    info_ref, in_ref, flag_ref, out_ref, near_ref, far_ref, m_ref, gx_ref, gy_ref, gz_ref, z_ref, edge_ref
):
    me = lax.axis_index("blocks")
    row, lane = iotas()

    def there(d):
        return jnp.full((8, 128), info_ref[0, d], jnp.int32) >= 0

    def arrived(key):
        chunk, place = GHOST[key]
        return in_ref[chunk * 40 + place * 8 : chunk * 40 + place * 8 + 8, :]

    def flags(x):
        return flag_ref[pl.ds(pl.multiple_of(x * 8, 8), 8), :]

    prepare_ghosts(
        lambda face, i: arrived((face, i)),
        arrived("EA"),
        arrived("EB"),
        there,
        gx_ref,
        gy_ref,
        gz_ref,
        lane,
    )

    def mask_plane(x, carry):
        loaded = []
        for i in range(19):
            chunk, place = tile_at(i, x)
            loaded.append(in_ref[pl.ds(pl.multiple_of(chunk * 40 + place * 8, 8), 8), :])
        for i, value in enumerate(masked(loaded, flags(x))):
            m_ref[tile_rows(i, x), :] = value
        return carry

    lax.fori_loop(0, 32, mask_plane, 0, unroll=4)

    def step(group, carry):
        faces = {}
        for part in range(4):
            x = group * 4 + part
            flag = flags(x)
            new = advance(
                x, lambda i, at: m_ref[tile_rows(i, at), :], gx_ref, gy_ref, gz_ref, flag == 0, row, lane
            )
            c = masked(collide(new), flag)
            for i in range(19):
                out_ref[tile_rows(i, x), :] = c[i]
            join_z_faces(c, x, faces, lane)
        store_z_faces(faces, group, z_ref, 0, lane)
        return carry

    lax.fori_loop(0, 8, step, 0)

    def plane(i, x):
        return out_ref[tile_rows(i, x), :]

    def load_rows(i, q, r):
        return out_ref[pl.ds((i * 32 + q) * 8 + r, 8, stride=32), :]

    y_face = {}
    for face in (2, 3):
        for i in FACE_PDFS[face]:
            y_face[i] = pack_y_face(load_rows, i, face, lane)
    edge_tile = pack_edges(plane, y_face, lane, edge_ref)
    edge_rows = edge_ref[...]
    for d in range(18):
        other = info_ref[0, d]
        cz = VELOCITY[d + 1][2]
        pair = (other >> 3) == (me >> 3)

        def send(ref, slot, d=d):
            def put(k, value):
                ref[pl.ds(pl.multiple_of(slot * 40 + k * 8, 8), 8), :] = value

            if d < 6:
                for k, i in enumerate(FACE_PDFS[d]):
                    if d < 2:
                        value = plane(i, 31 if d == 0 else 0)
                    elif d < 4:
                        value = y_face[i]
                    else:
                        n = Z_PDFS.index(i)
                        value = z_ref[8 * n : 8 * n + 8, :]
                    put(k, value)
            else:
                put(0, edge_tile)
                put(1, edge_rows)

        if cz == 0:

            @pl.when(other >= 0)
            def _():
                send(near_ref, other & 7)

        else:

            @pl.when((other >= 0) & pair)
            def _():
                send(near_ref, other & 7)

            @pl.when((other >= 0) & jnp.logical_not(pair))
            def _():
                send(far_ref, (other + 4) & 7)


def last_step_kernel(
    info_ref, in_ref, flag_ref, near_ref, far_ref, out_ref, gx_ref, gy_ref, gz_ref
):
    group = pl.program_id(0)
    me = lax.axis_index("blocks")
    row, lane = iotas()

    def there(d):
        return jnp.full((8, 128), info_ref[0, d], jnp.int32) >= 0

    def arrived(d, k):
        other = jnp.maximum(info_ref[0, d], 0)
        at = pl.ds(pl.multiple_of((other & 7) * 40 + k * 8, 8), 8)
        value = near_ref[at, :]
        if VELOCITY[d + 1][2]:
            pair = jnp.full((8, 128), (other >> 3) ^ (me >> 3), jnp.int32) == 0
            at = pl.ds(pl.multiple_of(((other + 4) & 7) * 40 + k * 8, 8), 8)
            value = jnp.where(pair, value, far_ref[at, :])
        return value

    @pl.when(group == 0)
    def _():
        edge_tile = jnp.zeros((8, 128), jnp.float32)
        for i in range(11, 19):
            edge_tile = jnp.where(lane % 32 == i - 11, arrived(opposite(i) - 1, 0), edge_tile)
        edge_rows = jnp.zeros((8, 128), jnp.float32)
        for i in range(7, 11):
            edge_rows = jnp.where(row == i - 7, arrived(opposite(i) - 1, 1), edge_rows)
        prepare_ghosts(
            lambda face, i: arrived(face ^ 1, FACE_PDFS[face].index(i)),
            edge_tile,
            edge_rows,
            there,
            gx_ref,
            gy_ref,
            gz_ref,
            lane,
        )

    for part in range(4):
        x = group * 4 + part
        fluid = flag_ref[pl.ds(pl.multiple_of(x * 8, 8), 8), :] == 0
        new = advance(
            x, lambda i, at: in_ref[tile_rows(i, at), :], gx_ref, gy_ref, gz_ref, fluid, row, lane
        )
        for i in range(19):
            out_ref[i, 8 * part : 8 * part + 8, :] = new[i]


F32 = jnp.float32
NEAR = [[8 * k + i for i in range(8)] for k in range(16)]
FAR = [[(8 * k + 4 + i) % 128 for i in range(8)] for k in range(16)]


def whole(shape):
    zeros = (0,) * len(shape)
    return pl.BlockSpec(shape, lambda *_: zeros)


def scratch(rows, dtype=F32):
    return pltpu.VMEM((rows, 128), dtype)


def array(*shape):
    return jax.ShapeDtypeStruct(shape, F32)


def mebibytes(n):
    return pltpu.CompilerParams(vmem_limit_bytes=n * 1024 * 1024)


def exchange(x, groups=None):
    return lax.all_to_all(
        x, "blocks", split_axis=0, concat_axis=0, axis_index_groups=groups, tiled=True
    )


def per_device(old_pdfs, old_slot, neighbours, cell_flags):
    flags = cell_flags.reshape(256, 128)
    smem = pl.BlockSpec(memory_space=pltpu.SMEM)
    vmem = pl.BlockSpec(memory_space=pltpu.VMEM)
    rows = old_pdfs.transpose(1, 0, 2).reshape(19, 2, 256, 128)
    rows = rows.transpose(0, 2, 1, 3).reshape(19, 512, 128)

    packed = pl.pallas_call(
        pack_kernel,
        grid=(8,),
        in_specs=[smem, smem, pl.BlockSpec((19, 64, 128), lambda g: (0, g, 0))],
        out_specs=pl.BlockSpec(memory_space=pl.ANY),
        out_shape=array(10240, 128),
        scratch_shapes=[
            scratch(10240),
            scratch(160),
            scratch(8),
            pltpu.SemaphoreType.DMA((25,)),
        ],
        compiler_params=mebibytes(16),
        name="pack",
    )(old_slot, neighbours, rows)
    spread = exchange(packed.reshape(128, 80, 128))

    picked = pl.pallas_call(
        pick_kernel,
        in_specs=[smem, vmem],
        out_specs=vmem,
        out_shape=array(5120, 128),
        scratch_shapes=[
            scratch(128, jnp.int32),
            pltpu.SMEM((128, 128), jnp.int32),
            pltpu.SemaphoreType.DMA,
        ],
        compiler_params=mebibytes(16),
        name="pick",
    )(old_slot, spread.reshape(10240, 128))
    arrived = exchange(picked.reshape(128, 40, 128))

    ghost_scratch = [scratch(80), scratch(2720), scratch(80)]
    state, near, far = pl.pallas_call(
        first_step_kernel,
        in_specs=[smem, vmem, vmem],
        out_specs=[vmem] * 3,
        out_shape=[array(4864, 128), array(320, 128), array(320, 128)],
        scratch_shapes=[scratch(4864)] + ghost_scratch + [scratch(80), scratch(8)],
        compiler_params=mebibytes(20),
        name="first_step",
    )(neighbours, arrived.reshape(5120, 128), flags)

    near = exchange(near.reshape(8, 40, 128), NEAR).reshape(320, 128)
    far = exchange(far.reshape(8, 40, 128), FAR).reshape(320, 128)

    new = pl.pallas_call(
        last_step_kernel,
        grid=(8,),
        in_specs=[smem, whole((4864, 128)), whole((256, 128)), whole((320, 128)), whole((320, 128))],
        out_specs=pl.BlockSpec((19, 32, 128), lambda g: (0, g, 0)),
        out_shape=array(19, 256, 128),
        scratch_shapes=ghost_scratch,
        compiler_params=mebibytes(16),
        name="last_step",
    )(neighbours, state, flags, near, far)
    return new.reshape(1, 19, 32768)


def solution(mesh):
    in_specs = (P("blocks", None, None), P(), P("blocks", None), P("blocks", None))
    return jax.shard_map(
        per_device,
        mesh=mesh,
        in_specs=in_specs,
        out_specs=P("blocks", None, None),
        check_vma=False,
    )
```

```python
import jax
import jax.numpy as jnp
from jax import lax
from jax.experimental import pallas as pl
from jax.experimental.pallas import tpu as pltpu
from jax.sharding import PartitionSpec as P

EDGE = 32
VELOCITY = (
    (0, 0, 0),
    (1, 0, 0),
    (-1, 0, 0),
    (0, 1, 0),
    (0, -1, 0),
    (0, 0, 1),
    (0, 0, -1),
    (1, 1, 0),
    (-1, -1, 0),
    (1, -1, 0),
    (-1, 1, 0),
    (1, 0, 1),
    (-1, 0, -1),
    (1, 0, -1),
    (-1, 0, 1),
    (0, 1, 1),
    (0, -1, -1),
    (0, 1, -1),
    (0, -1, 1),
)
WEIGHT = (1.0 / 3.0,) + (1.0 / 18.0,) * 6 + (1.0 / 36.0,) * 12
INLET = (0.0, 0.0, 0.05)
WALL = 1e30
OUTLET = 2e30

REST = [3, 4, 5, 6, 7, 8, 9, 10, 11, 12, 13, 14, 15, 16, 17, 18]
POSITION = {0: 7, 1: 11, 2: 15}
POSITION.update(
    zip(REST, [q for q in range(19) if q not in (7, 11, 15)])
)
FACE_PDFS = [
    [i for i in range(19) if VELOCITY[i][axis] == side]
    for axis in range(3)
    for side in (1, -1)
]
Y_PDFS = FACE_PDFS[2] + FACE_PDFS[3]
Z_PDFS = FACE_PDFS[4] + FACE_PDFS[5]
X_PDFS = FACE_PDFS[0] + FACE_PDFS[1]
CARRIERS = [(0, 7), (1, 10), (2, 7), (3, 9), (4, 15), (5, 17)]
TABLE_LANE = 104
EDGE_COLUMNS = [(12, 13), (11, 14), (16, 17), (15, 18)]


def opposite(i):
    return 0 if i == 0 else (i + 1 if i % 2 == 1 else i - 1)


def ghost_places():
    places = {}
    plain = [
        (f, i) for f in range(6) for i in FACE_PDFS[f] if (f, i) not in CARRIERS
    ]
    for n, item in enumerate(plain):
        places[item] = (120 + n // 3, 1 + n % 3)
    for n, item in enumerate(CARRIERS + ["EA", "EB"]):
        places[item] = (120 + n, 4)
    return places


GHOST = ghost_places()
EDGE_CHUNK = GHOST["EA"][0]
TABLE = [(d,) for d in range(6)]
TABLE += [tuple(opposite(i) - 1 for i in pdfs) for pdfs in EDGE_COLUMNS + [(7, 8, 9, 10)]]


def tile_at(i, x):
    pos = POSITION[i]
    chunk = (pos % 4) * 32 + x
    place = pos // 4
    if pos in (7, 11, 15):
        far = x >= 24
        if isinstance(x, int):
            if far:
                return 72 + 8 * ((pos - 7) // 4) + x, 4
            return chunk, place
        chunk = jnp.where(far, 72 + 8 * ((pos - 7) // 4) + x, chunk)
        place = jnp.where(far, 4, place)
    return chunk, place


def inlet_value(i):
    along = sum(c * v for c, v in zip(VELOCITY[i], INLET))
    square = sum(v * v for v in INLET)
    return WEIGHT[i] * (1.0 + 3.0 * along + 4.5 * along * along - 1.5 * square)


def iotas():
    row = lax.broadcasted_iota(jnp.int32, (8, 128), 0)
    lane = lax.broadcasted_iota(jnp.int32, (8, 128), 1)
    return row, lane


def momentum(f):
    jx = (f[1] - f[2]) + (f[7] - f[8]) + (f[9] - f[10]) + (f[11] - f[12]) + (f[13] - f[14])
    jy = (f[3] - f[4]) + (f[7] - f[8]) - (f[9] - f[10]) + (f[15] - f[16]) + (f[17] - f[18])
    jz = (f[5] - f[6]) + (f[11] - f[12]) - (f[13] - f[14]) + (f[15] - f[16]) - (f[17] - f[18])
    return jx, jy, jz


def collide(f):
    even = {i: f[i] + f[i + 1] for i in range(1, 19, 2)}
    odd = {i: f[i] - f[i + 1] for i in range(1, 19, 2)}
    x_xy, y_xy = odd[7] + odd[9], odd[7] - odd[9]
    x_xz, z_xz = odd[11] + odd[13], odd[11] - odd[13]
    y_yz, z_yz = odd[15] + odd[17], odd[15] - odd[17]
    edge_x, edge_y, edge_z = x_xy + x_xz, y_xy + y_yz, z_xz + z_yz
    jx, jy, jz = odd[1] + edge_x, odd[3] + edge_y, odd[5] + edge_z
    flux = [
        edge - 4.0 * axis + (2.0 / 3.0) * j
        for edge, axis, j in ((edge_x, odd[1], jx), (edge_y, odd[3], jy), (edge_z, odd[5], jz))
    ]
    third_x, third_y, third_z = x_xy - x_xz, y_xy - y_yz, z_xz - z_yz
    b_xy, b_xz, b_yz = even[7] + even[9], even[11] + even[13], even[15] + even[17]
    axes = even[1] + even[3] + even[5]
    edges = b_xy + b_xz + b_yz
    density = f[0] + axes + edges
    sx, sy, sz = jx * jx, jy * jy, jz * jz
    square = sx + sy + sz
    energy = -30.0 * f[0] - 11.0 * axes + 8.0 * edges + 11.0 * density - 19.0 * square
    fourth = 12.0 * f[0] - 4.0 * axes + edges - 3.0 * density + 5.5 * square
    rate_e, rate_f = 1.19 / 2394.0, 1.4 / 252.0
    out = [None] * 19
    out[0] = f[0] + (30.0 * rate_e) * energy - (12.0 * rate_f) * fourth
    axis_part = (11.0 * rate_e) * energy + (4.0 * rate_f) * fourth
    edge_part = (-8.0 * rate_e) * energy - rate_f * fourth
    axis_third, edge_third = axes * (1.0 / 3.0), edges * (1.0 / 3.0)
    third_square = square * (1.0 / 3.0)
    axis_delta, edge_delta = [], []
    for a, c, s in ((even[1], b_yz, sx), (even[3], b_xz, sy), (even[5], b_xy, sz)):
        alpha, gamma, tau = a - axis_third, c - edge_third, s - third_square
        p_mode = alpha - gamma - tau
        pi_mode = 0.5 * tau - 2.0 * alpha - gamma
        axis_delta.append(axis_part - (1.6 / 6.0) * p_mode + (2.8 / 12.0) * pi_mode)
        edge_delta.append(edge_part + (1.6 / 6.0) * p_mode + (1.4 / 12.0) * pi_mode)
    for k, i in enumerate((1, 3, 5)):
        odd_part = 0.12 * flux[k]
        out[i] = f[i] + (axis_delta[k] + odd_part)
        out[i + 1] = f[i + 1] + (axis_delta[k] - odd_part)
    fx, fy, fz = (0.03 * v for v in flux)
    hx, hy, hz = 0.2475 * third_x, 0.2475 * third_y, 0.2475 * third_z
    planes = (
        (7, 9, edge_delta[2], jx * jy, fx + hx, fy + hy),
        (11, 13, edge_delta[1], jx * jz, fx - hx, fz + hz),
        (15, 17, edge_delta[0], jy * jz, fy - hy, fz - hz),
    )
    for i, k, delta, cross, first, second in planes:
        shear = 0.4 * (even[i] - even[k] - cross)
        together, against = first + second, first - second
        same, mixed = delta - shear, delta + shear
        out[i] = f[i] + (same - together)
        out[i + 1] = f[i + 1] + (same + together)
        out[k] = f[k] + (mixed - against)
        out[k + 1] = f[k + 1] + (mixed + against)
    return out


def roll_lanes(v, shift):
    if isinstance(shift, int):
        shift = shift % 128
        return v if shift == 0 else pltpu.roll(v, shift, 1)
    return pltpu.roll(v, shift & 127, 1)


def pack_y_face(load_rows, i, face, lane):
    up = face == 2
    packed = None
    for q in range(4):
        rows = load_rows(i, q, 7 if up else 0)
        moved = roll_lanes(rows, 32 * q - 96 if up else 32 * q)
        packed = moved if packed is None else jnp.where((lane >> 5) == q, moved, packed)
    return packed


def join_z_faces(c, x, faces, lane):
    here = (lane & 31) == x
    for n, i in enumerate(Z_PDFS):
        moved = roll_lanes(c[i], x - (31 if n < 5 else 0) + 128)
        faces[n] = jnp.where(here, moved, faces[n]) if n in faces else moved


def store_z_faces(faces, group, z_ref, base, lane):
    here = (lane & 31) >> 2 == group
    for n in range(10):
        rows = slice(base + 8 * n, base + 8 * n + 8)
        z_ref[rows, :] = jnp.where(here, faces[n], z_ref[rows, :])


def pack_edges(plane, y_face, lane, edge_rows_ref):
    tile = jnp.zeros((8, 128), jnp.float32)
    for i in range(11, 19):
        cx, cy, cz = VELOCITY[i]
        source = plane(i, 31 if cx > 0 else 0) if cx else y_face[i]
        moved = roll_lanes(source, i - 11 - (31 if cz > 0 else 0))
        tile = jnp.where((lane & 31) == i - 11, moved, tile)
    edge_rows_ref[...] = jnp.zeros((8, 128), jnp.float32)
    for i in range(7, 11):
        cx, cy, _ = VELOCITY[i]
        line = plane(i, 31 if cx > 0 else 0)
        line = roll_lanes(line, 32 if cy > 0 else 0)
        row = 7 if cy > 0 else 0
        edge_rows_ref[i - 7 : i - 6, :] = line[row : row + 1, :]
    return tile


def pack_kernel(
    old_slot_hbm,
    neighbours_hbm,
    pdf_hbm,
    tiles_ref,
    pdf_ref,
    z_ref,
    edge_ref,
    old_slot_ref,
    neighbours_ref,
    sem_ref,
):
    row, lane = iotas()

    def fetch(g):
        rows = pl.ds(pl.multiple_of(g * 64, 64), 64)
        return pltpu.make_async_copy(pdf_hbm.at[:, rows], pdf_ref.at[:, rows], sem_ref.at[g])

    def fetch_indices():
        return (
            pltpu.make_async_copy(old_slot_hbm, old_slot_ref, sem_ref.at[8]),
            pltpu.make_async_copy(neighbours_hbm, neighbours_ref, sem_ref.at[9]),
        )

    for g in range(8):
        fetch(g).start()
    for copy in fetch_indices():
        copy.start()

    def rows_of(i, x, slot):
        chunk, place = tile_at(i, x)
        return chunk * 80 + slot * 40 + place * 8

    def planes(group, carry):
        fetch(group).wait()
        for slot in range(2):
            faces = {}
            for part in range(4):
                first = pl.multiple_of(group * 64, 64) + part * 16 + slot
                f = [pdf_ref[i, pl.ds(first, 8, stride=2), :] for i in range(19)]
                c = collide(f)
                x = group * 4 + part
                for i in range(19):
                    tiles_ref[pl.ds(pl.multiple_of(rows_of(i, x, slot), 8), 8), :] = c[i]
                join_z_faces(c, x, faces, lane)
            store_z_faces(faces, group, z_ref, 80 * slot, lane)
        return carry

    lax.fori_loop(0, 8, planes, 0)
    for copy in fetch_indices():
        copy.wait()
    table = jnp.zeros((8, 128), jnp.int32)
    for column, directions in enumerate(TABLE):
        other = jnp.int32(0)
        for d in directions:
            other = jnp.maximum(other, neighbours_ref[0, d])
        other = jnp.minimum(other, 127)
        table = jnp.where(lane == TABLE_LANE + column, old_slot_ref[other], table)
    table = table.astype(jnp.float32)
    free = (row == 7) & (lane >= TABLE_LANE) & (lane < TABLE_LANE + len(TABLE))

    def ghosts(slot, carry):
        def plane(i, x):
            return tiles_ref[pl.ds(pl.multiple_of(rows_of(i, x, slot), 8), 8), :]

        def load_rows(i, q, r):
            return tiles_ref[pl.ds(rows_of(i, q, slot) + r, 8, stride=320), :]

        def put(key, value):
            chunk, place = GHOST[key]
            if place == 4:
                value = jnp.where(free, table, value)
            at = pl.multiple_of(chunk * 80 + slot * 40 + place * 8, 8)
            tiles_ref[pl.ds(at, 8), :] = value

        for face in (0, 1):
            for i in FACE_PDFS[face]:
                put((face, i), plane(i, 31 if face == 0 else 0))
        y_face = {}
        for face in (2, 3):
            for i in FACE_PDFS[face]:
                y_face[i] = pack_y_face(load_rows, i, face, lane)
                put((face, i), y_face[i])
        for n, i in enumerate(Z_PDFS):
            face = 4 + n // 5
            put((face, i), z_ref[pl.ds(pl.multiple_of(80 * slot + 8 * n, 8), 8), :])
        put("EA", pack_edges(plane, y_face, lane, edge_ref))
        put("EB", edge_ref[...])
        return carry

    lax.fori_loop(0, 2, ghosts, 0)


def ghost_code(me, place):
    code = jnp.int32(0)
    for key, (chunk, at) in GHOST.items():
        if at == place and key != "EA":
            code = jnp.where(me == chunk, 10 if key == "EB" else key[0] ^ 1, code)
    return code


def pick_kernel(old_slot_ref, spread_ref, out_ref, table_ref, slots_ref, sem_ref):
    me = lax.axis_index("blocks")
    row, lane = iotas()

    def tile(slot, place):
        return spread_ref[pl.ds(pl.multiple_of(slot * 40 + place * 8, 8), 8), :]

    def store(n, place, value):
        out_ref[pl.ds(pl.multiple_of(n * 40 + place * 8, 8), 8), :] = value

    @pl.when(me < 120)
    def _():
        def own(n, carry):
            slot = old_slot_ref[n]
            for place in range(5):
                store(n, place, tile(slot, place))
            return carry

        lax.fori_loop(0, 128, own, 0, unroll=8)

    @pl.when(me >= 120)
    def _():
        for half in range(2):
            joined = None
            for u in range(8):
                rows = spread_ref[pl.ds((half * 8 + u) * 640 + 39, 8, stride=80), :]
                rows = roll_lanes(rows, 16 * u - TABLE_LANE)
                joined = rows if u == 0 else jnp.where(lane >> 4 == u, rows, joined)
            table_ref[8 * half : 8 * half + 8, :] = joined.astype(jnp.int32)
        copy = pltpu.make_async_copy(table_ref, slots_ref, sem_ref)
        copy.start()

        copy.wait()
        codes = [ghost_code(me, place) for place in range(5)]

        def loop(fourth):
            def body(b, carry):
                lane0 = (b & 7) * 16
                for r in range(8):
                    n = b * 8 + r
                    row0 = (b >> 3) * 8 + r
                    store(n, 0, tile(old_slot_ref[n], 0))
                    for place in range(1, 4):
                        store(n, place, tile(slots_ref[row0, lane0 + codes[place]], place))
                    fourth(n, row0, lane0)
                return carry

            lax.fori_loop(0, 16, body, 0)

        @pl.when(me != EDGE_CHUNK)
        def _():
            loop(lambda n, row0, lane0: store(n, 4, tile(slots_ref[row0, lane0 + codes[4]], 4)))

        @pl.when(me == EDGE_CHUNK)
        def _():
            z = lane & 31

            def merge(n, row0, lane0):
                value = None
                for column, pdfs in enumerate(EDGE_COLUMNS):
                    piece = tile(slots_ref[row0, lane0 + 6 + column], 4)
                    mask = (z == pdfs[0] - 11) | (z == pdfs[1] - 11)
                    value = piece if value is None else jnp.where(mask, piece, value)
                store(n, 4, value)

            loop(merge)


def prepare_ghosts(face_tile, edge_tile, edge_rows, there, gx_ref, gy_ref, gz_ref, lane):
    for n, i in enumerate(X_PDFS):
        face = n // 5
        gx_ref[8 * n : 8 * n + 8, :] = jnp.where(there(face ^ 1), face_tile(face, i), WALL)
    for n, i in enumerate(Z_PDFS):
        face = 4 + n // 5
        value = jnp.where(there(face ^ 1), face_tile(face, i), WALL)
        cx = VELOCITY[i][0]
        if cx:
            beyond = -1 if cx > 0 else 32
            line = roll_lanes(edge_tile, beyond - (i - 11))
            line = jnp.where(there(opposite(i) - 1), line, WALL)
            value = jnp.where((lane & 31) == beyond % 32, line, value)
        gz_ref[8 * n : 8 * n + 8, :] = value
    for n, i in enumerate(Y_PDFS):
        face = 2 + n // 5
        cx, cy, cz = VELOCITY[i]
        value = jnp.where(there(face ^ 1), face_tile(face, i), WALL)
        if cz:
            target = 0 if cz > 0 else 31
            line = roll_lanes(edge_tile, target - (i - 11))
            line = jnp.where(there(opposite(i) - 1), line, WALL)
            value = jnp.where((lane & 31) == target, line, roll_lanes(value, cz))
        r = 0 if cy > 0 else 7
        for q in range(4):
            moved = roll_lanes(value, (0 if cy > 0 else 96) - 32 * q)
            gy_ref[pl.ds(272 * n + (q + 1) * 8 + r, 8, stride=32), :] = moved
        if cx:
            line = jnp.where(there(opposite(i) - 1), edge_rows, WALL)
            line = roll_lanes(line, 0 if cy > 0 else 96)
            at = 272 * n + (0 if cx > 0 else 33 * 8) + r
            gy_ref[at : at + 1, :] = line[i - 7 : i - 6, :]


def advance(x, plane, gx_ref, gy_ref, gz_ref, fluid, row, lane):
    own = [plane(i, x) for i in range(19)]
    u = momentum(own)
    base = 1.0 - 1.5 * (u[0] * u[0] + u[1] * u[1] + u[2] * u[2])
    new = [jnp.where(fluid, own[0], 0.0)] + [None] * 18
    low, high = lane < 32, lane >= 96
    first, last = low & (row == 0), high & (row == 7)
    z = (lane & 31)
    for i in range(1, 19):
        cx, cy, cz = VELOCITY[i]
        if cx:
            inside = plane(i, jnp.clip(x - cx, 0, 31))
            n = X_PDFS.index(i)
            border = jnp.full((8, 128), x, jnp.int32) == (0 if cx > 0 else 31)
            source = jnp.where(border, gx_ref[8 * n : 8 * n + 8, :], inside)
        else:
            source = own[i]
        if cz:
            target = 0 if cz > 0 else 31
            n = Z_PDFS.index(i)
            ghost = roll_lanes(gz_ref[8 * n : 8 * n + 8, :], target - (x - cx) + 128)
            source = jnp.where(z == target, ghost, roll_lanes(source, cz))
        if cy:
            n = Y_PDFS.index(i)
            ghost = gy_ref[pl.ds(pl.multiple_of(272 * n + (x - cx + 1) * 8, 8), 8), :]
            turned = roll_lanes(source, 32 * cy)
            carried = pltpu.roll(turned, cy % 8, 0)
            source = jnp.where(low if cy > 0 else high, carried, turned)
            source = jnp.where(first if cy > 0 else last, ghost, source)
        new[i] = source
    for i in range(1, 19, 2):
        cx, cy, cz = VELOCITY[i]
        along = None
        for c, v in zip((cx, cy, cz), u):
            if c:
                along = v * float(c) if along is None else (along + v if c > 0 else along - v)
        even = WEIGHT[i] * (base + 4.5 * along * along)
        odd = (3.0 * WEIGHT[i]) * along
        for k, outlet, bounce in ((i, even + odd, own[i + 1]), (i + 1, even - odd, own[i])):
            value = jnp.where(new[k] < 1.5e30, bounce, outlet)
            value = jnp.where(new[k] < 1e29, new[k], value)
            new[k] = jnp.where(fluid, value, 0.0)
    return new


def masked(c, flag):
    fluid, inlet = flag == 0, flag == 2
    sentinel = jnp.where(flag == 1, WALL, OUTLET)
    return [c[0]] + [
        jnp.where(fluid, c[i], jnp.where(inlet, inlet_value(i), sentinel)) for i in range(1, 19)
    ]


def tile_rows(i, x):
    return pl.ds(pl.multiple_of((i * 32 + x) * 8, 8), 8)


def first_step_kernel(
    info_ref, in_ref, flag_ref, out_ref, near_ref, far_ref, m_ref, gx_ref, gy_ref, gz_ref, z_ref, edge_ref
):
    me = lax.axis_index("blocks")
    row, lane = iotas()

    def there(d):
        return jnp.full((8, 128), info_ref[0, d], jnp.int32) >= 0

    def arrived(key):
        chunk, place = GHOST[key]
        return in_ref[chunk * 40 + place * 8 : chunk * 40 + place * 8 + 8, :]

    def flags(x):
        return flag_ref[pl.ds(pl.multiple_of(x * 8, 8), 8), :]

    prepare_ghosts(
        lambda face, i: arrived((face, i)),
        arrived("EA"),
        arrived("EB"),
        there,
        gx_ref,
        gy_ref,
        gz_ref,
        lane,
    )

    def mask_plane(x, carry):
        loaded = []
        for i in range(19):
            chunk, place = tile_at(i, x)
            loaded.append(in_ref[pl.ds(pl.multiple_of(chunk * 40 + place * 8, 8), 8), :])
        for i, value in enumerate(masked(loaded, flags(x))):
            m_ref[tile_rows(i, x), :] = value
        return carry

    lax.fori_loop(0, 32, mask_plane, 0, unroll=4)

    def step(group, carry):
        faces = {}
        for part in range(4):
            x = group * 4 + part
            flag = flags(x)
            new = advance(
                x, lambda i, at: m_ref[tile_rows(i, at), :], gx_ref, gy_ref, gz_ref, flag == 0, row, lane
            )
            c = masked(collide(new), flag)
            for i in range(19):
                out_ref[tile_rows(i, x), :] = c[i]
            join_z_faces(c, x, faces, lane)
        store_z_faces(faces, group, z_ref, 0, lane)
        return carry

    lax.fori_loop(0, 8, step, 0)

    def plane(i, x):
        return out_ref[tile_rows(i, x), :]

    def load_rows(i, q, r):
        return out_ref[pl.ds((i * 32 + q) * 8 + r, 8, stride=32), :]

    y_face = {}
    for face in (2, 3):
        for i in FACE_PDFS[face]:
            y_face[i] = pack_y_face(load_rows, i, face, lane)
    edge_tile = pack_edges(plane, y_face, lane, edge_ref)
    edge_rows = edge_ref[...]
    for d in range(18):
        other = info_ref[0, d]
        cz = VELOCITY[d + 1][2]
        pair = (other >> 3) == (me >> 3)

        def send(ref, slot, d=d):
            def put(k, value):
                ref[pl.ds(pl.multiple_of(slot * 40 + k * 8, 8), 8), :] = value

            if d < 6:
                for k, i in enumerate(FACE_PDFS[d]):
                    if d < 2:
                        value = plane(i, 31 if d == 0 else 0)
                    elif d < 4:
                        value = y_face[i]
                    else:
                        n = Z_PDFS.index(i)
                        value = z_ref[8 * n : 8 * n + 8, :]
                    put(k, value)
            else:
                put(0, edge_tile)
                put(1, edge_rows)

        if cz == 0:

            @pl.when(other >= 0)
            def _():
                send(near_ref, other & 7)

        else:

            @pl.when((other >= 0) & pair)
            def _():
                send(near_ref, other & 7)

            @pl.when((other >= 0) & jnp.logical_not(pair))
            def _():
                send(far_ref, (other + 4) & 7)


def last_step_kernel(
    info_ref, in_ref, flag_ref, near_ref, far_ref, out_hbm, out_ref, gx_ref, gy_ref, gz_ref, sem_ref
):
    me = lax.axis_index("blocks")
    row, lane = iotas()

    def there(d):
        return jnp.full((8, 128), info_ref[0, d], jnp.int32) >= 0

    def arrived(d, k):
        other = jnp.maximum(info_ref[0, d], 0)
        at = pl.ds(pl.multiple_of((other & 7) * 40 + k * 8, 8), 8)
        value = near_ref[at, :]
        if VELOCITY[d + 1][2]:
            pair = jnp.full((8, 128), (other >> 3) ^ (me >> 3), jnp.int32) == 0
            at = pl.ds(pl.multiple_of(((other + 4) & 7) * 40 + k * 8, 8), 8)
            value = jnp.where(pair, value, far_ref[at, :])
        return value

    edge_tile = jnp.zeros((8, 128), jnp.float32)
    for i in range(11, 19):
        edge_tile = jnp.where((lane & 31) == i - 11, arrived(opposite(i) - 1, 0), edge_tile)
    edge_rows = jnp.zeros((8, 128), jnp.float32)
    for i in range(7, 11):
        edge_rows = jnp.where(row == i - 7, arrived(opposite(i) - 1, 1), edge_rows)
    prepare_ghosts(
        lambda face, i: arrived(face ^ 1, FACE_PDFS[face].index(i)),
        edge_tile,
        edge_rows,
        there,
        gx_ref,
        gy_ref,
        gz_ref,
        lane,
    )

    def send(group):
        rows = pl.ds(pl.multiple_of(group * 32, 32), 32)
        return pltpu.make_async_copy(out_ref.at[:, rows], out_hbm.at[:, rows], sem_ref.at[group])

    def planes(group, carry):
        for part in range(4):
            x = group * 4 + part
            at = pl.ds(pl.multiple_of(x * 8, 8), 8)
            fluid = flag_ref[at, :] == 0
            new = advance(
                x, lambda i, at: in_ref[tile_rows(i, at), :], gx_ref, gy_ref, gz_ref, fluid, row, lane
            )
            for i in range(19):
                out_ref[i, at, :] = new[i]
        send(group).start()
        return carry

    lax.fori_loop(0, 8, planes, 0)
    for group in range(8):
        send(group).wait()


F32 = jnp.float32
NEAR = [[8 * k + i for i in range(8)] for k in range(16)]
FAR = [[(8 * k + 4 + i) % 128 for i in range(8)] for k in range(16)]


def scratch(rows, dtype=F32):
    return pltpu.VMEM((rows, 128), dtype)


def array(*shape):
    return jax.ShapeDtypeStruct(shape, F32)


def mebibytes(n):
    return pltpu.CompilerParams(vmem_limit_bytes=n * 1024 * 1024)


def exchange(x, groups=None):
    return lax.all_to_all(
        x, "blocks", split_axis=0, concat_axis=0, axis_index_groups=groups, tiled=True
    )


def per_device(old_pdfs, old_slot, neighbours, cell_flags):
    flags = cell_flags.reshape(256, 128)
    smem = pl.BlockSpec(memory_space=pltpu.SMEM)
    vmem = pl.BlockSpec(memory_space=pltpu.VMEM)
    rows = old_pdfs.transpose(1, 0, 2).reshape(19, 2, 256, 128)
    rows = rows.transpose(0, 2, 1, 3).reshape(19, 512, 128)

    hbm = pl.BlockSpec(memory_space=pltpu.HBM)
    packed = pl.pallas_call(
        pack_kernel,
        in_specs=[hbm] * 3,
        out_specs=vmem,
        out_shape=array(10240, 128),
        scratch_shapes=[
            pltpu.VMEM((19, 512, 128), F32),
            scratch(160),
            scratch(8),
            pltpu.SMEM((128,), jnp.int32),
            pltpu.SMEM((1, 18), jnp.int32),
            pltpu.SemaphoreType.DMA((10,)),
        ],
        compiler_params=mebibytes(24),
        name="pack",
    )(*(pltpu.with_memory_space_constraint(x, pltpu.HBM) for x in (old_slot, neighbours, rows)))
    spread = exchange(packed.reshape(128, 80, 128))

    picked = pl.pallas_call(
        pick_kernel,
        in_specs=[smem, vmem],
        out_specs=vmem,
        out_shape=array(5120, 128),
        scratch_shapes=[
            scratch(16, jnp.int32),
            pltpu.SMEM((16, 128), jnp.int32),
            pltpu.SemaphoreType.DMA,
        ],
        compiler_params=mebibytes(16),
        name="pick",
    )(old_slot, spread.reshape(10240, 128))
    arrived = exchange(picked.reshape(128, 40, 128))

    ghost_scratch = [scratch(80), scratch(2720), scratch(80)]
    state, near, far = pl.pallas_call(
        first_step_kernel,
        in_specs=[smem, vmem, vmem],
        out_specs=[vmem] * 3,
        out_shape=[array(4864, 128), array(320, 128), array(320, 128)],
        scratch_shapes=[scratch(4864)] + ghost_scratch + [scratch(80), scratch(8)],
        compiler_params=mebibytes(20),
        name="first_step",
    )(neighbours, arrived.reshape(5120, 128), flags)

    near = exchange(near.reshape(8, 40, 128), NEAR).reshape(320, 128)
    far = exchange(far.reshape(8, 40, 128), FAR).reshape(320, 128)

    new = pl.pallas_call(
        last_step_kernel,
        in_specs=[smem, vmem, vmem, vmem, vmem],
        out_specs=hbm,
        out_shape=array(19, 256, 128),
        scratch_shapes=[pltpu.VMEM((19, 256, 128), F32)]
        + ghost_scratch
        + [pltpu.SemaphoreType.DMA((8,))],
        compiler_params=mebibytes(16),
        name="last_step",
    )(neighbours, state, flags, near, far)
    return new.reshape(1, 19, 32768)


def solution(mesh):
    in_specs = (P("blocks", None, None), P(), P("blocks", None), P("blocks", None))
    return jax.shard_map(
        per_device,
        mesh=mesh,
        in_specs=in_specs,
        out_specs=P("blocks", None, None),
        check_vma=False,
    )
```

```python
import jax
import jax.numpy as jnp
from jax import lax
from jax.experimental import pallas as pl
from jax.experimental.pallas import tpu as pltpu
from jax.sharding import PartitionSpec as P

EDGE = 32
VELOCITY = (
    (0, 0, 0),
    (1, 0, 0),
    (-1, 0, 0),
    (0, 1, 0),
    (0, -1, 0),
    (0, 0, 1),
    (0, 0, -1),
    (1, 1, 0),
    (-1, -1, 0),
    (1, -1, 0),
    (-1, 1, 0),
    (1, 0, 1),
    (-1, 0, -1),
    (1, 0, -1),
    (-1, 0, 1),
    (0, 1, 1),
    (0, -1, -1),
    (0, 1, -1),
    (0, -1, 1),
)
WEIGHT = (1.0 / 3.0,) + (1.0 / 18.0,) * 6 + (1.0 / 36.0,) * 12
INLET = (0.0, 0.0, 0.05)
WALL = 1e30
OUTLET = 2e30

REST = [3, 4, 5, 6, 7, 8, 9, 10, 11, 12, 13, 14, 15, 16, 17, 18]
POSITION = {0: 7, 1: 11, 2: 15}
POSITION.update(
    zip(REST, [q for q in range(19) if q not in (7, 11, 15)])
)
FACE_PDFS = [
    [i for i in range(19) if VELOCITY[i][axis] == side]
    for axis in range(3)
    for side in (1, -1)
]
Y_PDFS = FACE_PDFS[2] + FACE_PDFS[3]
Z_PDFS = FACE_PDFS[4] + FACE_PDFS[5]
X_PDFS = FACE_PDFS[0] + FACE_PDFS[1]
CARRIERS = [(0, 7), (1, 10), (2, 7), (3, 9), (4, 15), (5, 17)]
TABLE_LANE = 104
EDGE_COLUMNS = [(12, 13), (11, 14), (16, 17), (15, 18)]


def opposite(i):
    return 0 if i == 0 else (i + 1 if i % 2 == 1 else i - 1)


def ghost_places():
    places = {}
    plain = [
        (f, i) for f in range(6) for i in FACE_PDFS[f] if (f, i) not in CARRIERS
    ]
    for n, item in enumerate(plain):
        places[item] = (120 + n // 3, 1 + n % 3)
    for n, item in enumerate(CARRIERS + ["EA", "EB"]):
        places[item] = (120 + n, 4)
    return places


GHOST = ghost_places()
EDGE_CHUNK = GHOST["EA"][0]
TABLE = [(d,) for d in range(6)]
TABLE += [tuple(opposite(i) - 1 for i in pdfs) for pdfs in EDGE_COLUMNS + [(7, 8, 9, 10)]]


def tile_at(i, x):
    pos = POSITION[i]
    chunk = (pos % 4) * 32 + x
    place = pos // 4
    if pos in (7, 11, 15):
        far = x >= 24
        if isinstance(x, int):
            if far:
                return 72 + 8 * ((pos - 7) // 4) + x, 4
            return chunk, place
        chunk = jnp.where(far, 72 + 8 * ((pos - 7) // 4) + x, chunk)
        place = jnp.where(far, 4, place)
    return chunk, place


def inlet_value(i):
    along = sum(c * v for c, v in zip(VELOCITY[i], INLET))
    square = sum(v * v for v in INLET)
    return WEIGHT[i] * (1.0 + 3.0 * along + 4.5 * along * along - 1.5 * square)


def iotas():
    row = lax.broadcasted_iota(jnp.int32, (8, 128), 0)
    lane = lax.broadcasted_iota(jnp.int32, (8, 128), 1)
    return row, lane


def momentum(f):
    jx = (f[1] - f[2]) + (f[7] - f[8]) + (f[9] - f[10]) + (f[11] - f[12]) + (f[13] - f[14])
    jy = (f[3] - f[4]) + (f[7] - f[8]) - (f[9] - f[10]) + (f[15] - f[16]) + (f[17] - f[18])
    jz = (f[5] - f[6]) + (f[11] - f[12]) - (f[13] - f[14]) + (f[15] - f[16]) - (f[17] - f[18])
    return jx, jy, jz


def collide(f):
    even = {i: f[i] + f[i + 1] for i in range(1, 19, 2)}
    odd = {i: f[i] - f[i + 1] for i in range(1, 19, 2)}
    x_xy, y_xy = odd[7] + odd[9], odd[7] - odd[9]
    x_xz, z_xz = odd[11] + odd[13], odd[11] - odd[13]
    y_yz, z_yz = odd[15] + odd[17], odd[15] - odd[17]
    edge_x, edge_y, edge_z = x_xy + x_xz, y_xy + y_yz, z_xz + z_yz
    jx, jy, jz = odd[1] + edge_x, odd[3] + edge_y, odd[5] + edge_z
    flux = [
        edge - 4.0 * axis + (2.0 / 3.0) * j
        for edge, axis, j in ((edge_x, odd[1], jx), (edge_y, odd[3], jy), (edge_z, odd[5], jz))
    ]
    third_x, third_y, third_z = x_xy - x_xz, y_xy - y_yz, z_xz - z_yz
    b_xy, b_xz, b_yz = even[7] + even[9], even[11] + even[13], even[15] + even[17]
    axes = even[1] + even[3] + even[5]
    edges = b_xy + b_xz + b_yz
    density = f[0] + axes + edges
    sx, sy, sz = jx * jx, jy * jy, jz * jz
    square = sx + sy + sz
    energy = -30.0 * f[0] - 11.0 * axes + 8.0 * edges + 11.0 * density - 19.0 * square
    fourth = 12.0 * f[0] - 4.0 * axes + edges - 3.0 * density + 5.5 * square
    rate_e, rate_f = 1.19 / 2394.0, 1.4 / 252.0
    out = [None] * 19
    out[0] = f[0] + (30.0 * rate_e) * energy - (12.0 * rate_f) * fourth
    axis_part = (11.0 * rate_e) * energy + (4.0 * rate_f) * fourth
    edge_part = (-8.0 * rate_e) * energy - rate_f * fourth
    axis_third, edge_third = axes * (1.0 / 3.0), edges * (1.0 / 3.0)
    third_square = square * (1.0 / 3.0)
    axis_delta, edge_delta = [], []
    for a, c, s in ((even[1], b_yz, sx), (even[3], b_xz, sy), (even[5], b_xy, sz)):
        alpha, gamma, tau = a - axis_third, c - edge_third, s - third_square
        p_mode = alpha - gamma - tau
        pi_mode = 0.5 * tau - 2.0 * alpha - gamma
        axis_delta.append(axis_part - (1.6 / 6.0) * p_mode + (2.8 / 12.0) * pi_mode)
        edge_delta.append(edge_part + (1.6 / 6.0) * p_mode + (1.4 / 12.0) * pi_mode)
    for k, i in enumerate((1, 3, 5)):
        odd_part = 0.12 * flux[k]
        out[i] = f[i] + (axis_delta[k] + odd_part)
        out[i + 1] = f[i + 1] + (axis_delta[k] - odd_part)
    fx, fy, fz = (0.03 * v for v in flux)
    hx, hy, hz = 0.2475 * third_x, 0.2475 * third_y, 0.2475 * third_z
    planes = (
        (7, 9, edge_delta[2], jx * jy, fx + hx, fy + hy),
        (11, 13, edge_delta[1], jx * jz, fx - hx, fz + hz),
        (15, 17, edge_delta[0], jy * jz, fy - hy, fz - hz),
    )
    for i, k, delta, cross, first, second in planes:
        shear = 0.4 * (even[i] - even[k] - cross)
        together, against = first + second, first - second
        same, mixed = delta - shear, delta + shear
        out[i] = f[i] + (same - together)
        out[i + 1] = f[i + 1] + (same + together)
        out[k] = f[k] + (mixed - against)
        out[k + 1] = f[k + 1] + (mixed + against)
    return out


def roll_lanes(v, shift):
    if isinstance(shift, int):
        shift = shift % 128
        return v if shift == 0 else pltpu.roll(v, shift, 1)
    return pltpu.roll(v, shift & 127, 1)


def pack_y_face(load_rows, i, face, lane):
    up = face == 2
    packed = None
    for q in range(4):
        rows = load_rows(i, q, 7 if up else 0)
        moved = roll_lanes(rows, 32 * q - 96 if up else 32 * q)
        packed = moved if packed is None else jnp.where((lane >> 5) == q, moved, packed)
    return packed


def join_z_faces(c, x, faces, lane):
    here = (lane & 31) == x
    for n, i in enumerate(Z_PDFS):
        moved = roll_lanes(c[i], x - (31 if n < 5 else 0) + 128)
        faces[n] = jnp.where(here, moved, faces[n]) if n in faces else moved


def store_z_faces(faces, group, z_ref, base, lane):
    here = (lane & 31) >> 2 == group
    for n in range(10):
        rows = slice(base + 8 * n, base + 8 * n + 8)
        z_ref[rows, :] = jnp.where(here, faces[n], z_ref[rows, :])


def pack_edges(plane, y_face, lane, edge_rows_ref):
    tile = jnp.zeros((8, 128), jnp.float32)
    for i in range(11, 19):
        cx, cy, cz = VELOCITY[i]
        source = plane(i, 31 if cx > 0 else 0) if cx else y_face[i]
        moved = roll_lanes(source, i - 11 - (31 if cz > 0 else 0))
        tile = jnp.where((lane & 31) == i - 11, moved, tile)
    edge_rows_ref[...] = jnp.zeros((8, 128), jnp.float32)
    for i in range(7, 11):
        cx, cy, _ = VELOCITY[i]
        line = plane(i, 31 if cx > 0 else 0)
        line = roll_lanes(line, 32 if cy > 0 else 0)
        row = 7 if cy > 0 else 0
        edge_rows_ref[i - 7 : i - 6, :] = line[row : row + 1, :]
    return tile


def pack_kernel(
    old_slot_hbm,
    neighbours_hbm,
    pdf_hbm,
    tiles_ref,
    pdf_ref,
    z_ref,
    edge_ref,
    old_slot_ref,
    neighbours_ref,
    sem_ref,
):
    row, lane = iotas()

    def fetch(g):
        rows = pl.ds(pl.multiple_of(g * 64, 64), 64)
        return pltpu.make_async_copy(pdf_hbm.at[:, rows], pdf_ref.at[:, rows], sem_ref.at[g])

    def fetch_indices():
        return (
            pltpu.make_async_copy(old_slot_hbm, old_slot_ref, sem_ref.at[8]),
            pltpu.make_async_copy(neighbours_hbm, neighbours_ref, sem_ref.at[9]),
        )

    for g in range(8):
        fetch(g).start()
    for copy in fetch_indices():
        copy.start()

    def rows_of(i, x, slot):
        chunk, place = tile_at(i, x)
        return chunk * 80 + slot * 40 + place * 8

    def planes(group, carry):
        fetch(group).wait()
        for slot in range(2):
            faces = {}
            for part in range(4):
                first = pl.multiple_of(group * 64, 64) + part * 16 + slot
                f = [pdf_ref[i, pl.ds(first, 8, stride=2), :] for i in range(19)]
                c = collide(f)
                x = group * 4 + part
                for i in range(19):
                    tiles_ref[pl.ds(pl.multiple_of(rows_of(i, x, slot), 8), 8), :] = c[i]
                join_z_faces(c, x, faces, lane)
            store_z_faces(faces, group, z_ref, 80 * slot, lane)
        return carry

    lax.fori_loop(0, 8, planes, 0)
    for copy in fetch_indices():
        copy.wait()
    table = jnp.zeros((8, 128), jnp.int32)
    for column, directions in enumerate(TABLE):
        other = jnp.int32(0)
        for d in directions:
            other = jnp.maximum(other, neighbours_ref[0, d])
        other = jnp.minimum(other, 127)
        table = jnp.where(lane == TABLE_LANE + column, old_slot_ref[other], table)
    table = table.astype(jnp.float32)
    free = (row == 7) & (lane >= TABLE_LANE) & (lane < TABLE_LANE + len(TABLE))

    def ghosts(slot, carry):
        def plane(i, x):
            return tiles_ref[pl.ds(pl.multiple_of(rows_of(i, x, slot), 8), 8), :]

        def load_rows(i, q, r):
            return tiles_ref[pl.ds(rows_of(i, q, slot) + r, 8, stride=320), :]

        def put(key, value):
            chunk, place = GHOST[key]
            if place == 4:
                value = jnp.where(free, table, value)
            at = pl.multiple_of(chunk * 80 + slot * 40 + place * 8, 8)
            tiles_ref[pl.ds(at, 8), :] = value

        for face in (0, 1):
            for i in FACE_PDFS[face]:
                put((face, i), plane(i, 31 if face == 0 else 0))
        y_face = {}
        for face in (2, 3):
            for i in FACE_PDFS[face]:
                y_face[i] = pack_y_face(load_rows, i, face, lane)
                put((face, i), y_face[i])
        for n, i in enumerate(Z_PDFS):
            face = 4 + n // 5
            put((face, i), z_ref[pl.ds(pl.multiple_of(80 * slot + 8 * n, 8), 8), :])
        put("EA", pack_edges(plane, y_face, lane, edge_ref))
        put("EB", edge_ref[...])
        return carry

    lax.fori_loop(0, 2, ghosts, 0)


def ghost_code(me, place):
    code = jnp.int32(0)
    for key, (chunk, at) in GHOST.items():
        if at == place and key != "EA":
            code = jnp.where(me == chunk, 10 if key == "EB" else key[0] ^ 1, code)
    return code


def pick_kernel(old_slot_ref, spread_ref, out_ref, table_ref, slots_ref, sem_ref):
    me = lax.axis_index("blocks")
    row, lane = iotas()

    def tile(slot, place):
        return spread_ref[pl.ds(pl.multiple_of(slot * 40 + place * 8, 8), 8), :]

    def store(n, place, value):
        out_ref[pl.ds(pl.multiple_of(n * 40 + place * 8, 8), 8), :] = value

    @pl.when(me < 120)
    def _():
        def own(n, carry):
            slot = old_slot_ref[n]
            for place in range(5):
                store(n, place, tile(slot, place))
            return carry

        lax.fori_loop(0, 128, own, 0, unroll=8)

    @pl.when(me >= 120)
    def _():
        for half in range(2):
            joined = None
            for u in range(8):
                rows = spread_ref[pl.ds((half * 8 + u) * 640 + 39, 8, stride=80), :]
                rows = roll_lanes(rows, 16 * u - TABLE_LANE)
                joined = rows if u == 0 else jnp.where(lane >> 4 == u, rows, joined)
            table_ref[8 * half : 8 * half + 8, :] = joined.astype(jnp.int32)
        copy = pltpu.make_async_copy(table_ref, slots_ref, sem_ref)
        copy.start()


        def own(n, carry):
            store(n, 0, tile(old_slot_ref[n], 0))
            return carry

        lax.fori_loop(0, 128, own, 0, unroll=16)
        copy.wait()
        codes = [ghost_code(me, place) for place in range(5)]

        def loop(fourth):
            def body(b, carry):
                lane0 = (b & 7) * 16
                for r in range(8):
                    n = b * 8 + r
                    row0 = (b >> 3) * 8 + r
                    for place in range(1, 4):
                        store(n, place, tile(slots_ref[row0, lane0 + codes[place]], place))
                    fourth(n, row0, lane0)
                return carry

            lax.fori_loop(0, 16, body, 0)

        @pl.when(me != EDGE_CHUNK)
        def _():
            loop(lambda n, row0, lane0: store(n, 4, tile(slots_ref[row0, lane0 + codes[4]], 4)))

        @pl.when(me == EDGE_CHUNK)
        def _():
            z = lane & 31

            def merge(n, row0, lane0):
                value = None
                for column, pdfs in enumerate(EDGE_COLUMNS):
                    piece = tile(slots_ref[row0, lane0 + 6 + column], 4)
                    mask = (z == pdfs[0] - 11) | (z == pdfs[1] - 11)
                    value = piece if value is None else jnp.where(mask, piece, value)
                store(n, 4, value)

            loop(merge)


def prepare_ghosts(face_tile, edge_tile, edge_rows, there, gx_ref, gy_ref, gz_ref, lane):
    for n, i in enumerate(X_PDFS):
        face = n // 5
        gx_ref[8 * n : 8 * n + 8, :] = jnp.where(there(face ^ 1), face_tile(face, i), WALL)
    for n, i in enumerate(Z_PDFS):
        face = 4 + n // 5
        value = jnp.where(there(face ^ 1), face_tile(face, i), WALL)
        cx = VELOCITY[i][0]
        if cx:
            beyond = -1 if cx > 0 else 32
            line = roll_lanes(edge_tile, beyond - (i - 11))
            line = jnp.where(there(opposite(i) - 1), line, WALL)
            value = jnp.where((lane & 31) == beyond % 32, line, value)
        gz_ref[8 * n : 8 * n + 8, :] = value
    for n, i in enumerate(Y_PDFS):
        face = 2 + n // 5
        cx, cy, cz = VELOCITY[i]
        value = jnp.where(there(face ^ 1), face_tile(face, i), WALL)
        if cz:
            target = 0 if cz > 0 else 31
            line = roll_lanes(edge_tile, target - (i - 11))
            line = jnp.where(there(opposite(i) - 1), line, WALL)
            value = jnp.where((lane & 31) == target, line, roll_lanes(value, cz))
        r = 0 if cy > 0 else 7
        for q in range(4):
            moved = roll_lanes(value, (0 if cy > 0 else 96) - 32 * q)
            gy_ref[pl.ds(272 * n + (q + 1) * 8 + r, 8, stride=32), :] = moved
        if cx:
            line = jnp.where(there(opposite(i) - 1), edge_rows, WALL)
            line = roll_lanes(line, 0 if cy > 0 else 96)
            at = 272 * n + (0 if cx > 0 else 33 * 8) + r
            gy_ref[at : at + 1, :] = line[i - 7 : i - 6, :]


def advance(x, plane, gx_ref, gy_ref, gz_ref, fluid, row, lane):
    own = [plane(i, x) for i in range(19)]
    u = momentum(own)
    base = 1.0 - 1.5 * (u[0] * u[0] + u[1] * u[1] + u[2] * u[2])
    new = [jnp.where(fluid, own[0], 0.0)] + [None] * 18
    low, high = lane < 32, lane >= 96
    first, last = low & (row == 0), high & (row == 7)
    z = (lane & 31)
    for i in range(1, 19):
        cx, cy, cz = VELOCITY[i]
        if cx:
            inside = plane(i, jnp.clip(x - cx, 0, 31))
            n = X_PDFS.index(i)
            border = jnp.full((8, 128), x, jnp.int32) == (0 if cx > 0 else 31)
            source = jnp.where(border, gx_ref[8 * n : 8 * n + 8, :], inside)
        else:
            source = own[i]
        if cz:
            target = 0 if cz > 0 else 31
            n = Z_PDFS.index(i)
            ghost = roll_lanes(gz_ref[8 * n : 8 * n + 8, :], target - (x - cx) + 128)
            source = jnp.where(z == target, ghost, roll_lanes(source, cz))
        if cy:
            n = Y_PDFS.index(i)
            ghost = gy_ref[pl.ds(pl.multiple_of(272 * n + (x - cx + 1) * 8, 8), 8), :]
            turned = roll_lanes(source, 32 * cy)
            carried = pltpu.roll(turned, cy % 8, 0)
            source = jnp.where(low if cy > 0 else high, carried, turned)
            source = jnp.where(first if cy > 0 else last, ghost, source)
        new[i] = source
    for i in range(1, 19, 2):
        cx, cy, cz = VELOCITY[i]
        along = None
        for c, v in zip((cx, cy, cz), u):
            if c:
                along = v * float(c) if along is None else (along + v if c > 0 else along - v)
        even = WEIGHT[i] * (base + 4.5 * along * along)
        odd = (3.0 * WEIGHT[i]) * along
        for k, outlet, bounce in ((i, even + odd, own[i + 1]), (i + 1, even - odd, own[i])):
            value = jnp.where(new[k] < 1.5e30, bounce, outlet)
            value = jnp.where(new[k] < 1e29, new[k], value)
            new[k] = jnp.where(fluid, value, 0.0)
    return new


def masked(c, flag):
    fluid, inlet = flag == 0, flag == 2
    sentinel = jnp.where(flag == 1, WALL, OUTLET)
    return [c[0]] + [
        jnp.where(fluid, c[i], jnp.where(inlet, inlet_value(i), sentinel)) for i in range(1, 19)
    ]


def tile_rows(i, x):
    return pl.ds(pl.multiple_of((i * 32 + x) * 8, 8), 8)


def first_step_kernel(
    info_ref, in_ref, flag_ref, out_ref, side_ref, up_ref, down_ref, m_ref, gx_ref, gy_ref, gz_ref, z_ref, edge_ref
):
    row, lane = iotas()

    def there(d):
        return jnp.full((8, 128), info_ref[0, d], jnp.int32) >= 0

    def arrived(key):
        chunk, place = GHOST[key]
        return in_ref[chunk * 40 + place * 8 : chunk * 40 + place * 8 + 8, :]

    def flags(x):
        return flag_ref[pl.ds(pl.multiple_of(x * 8, 8), 8), :]

    prepare_ghosts(
        lambda face, i: arrived((face, i)),
        arrived("EA"),
        arrived("EB"),
        there,
        gx_ref,
        gy_ref,
        gz_ref,
        lane,
    )

    def mask_plane(x, carry):
        loaded = []
        for i in range(19):
            chunk, place = tile_at(i, x)
            loaded.append(in_ref[pl.ds(pl.multiple_of(chunk * 40 + place * 8, 8), 8), :])
        for i, value in enumerate(masked(loaded, flags(x))):
            m_ref[tile_rows(i, x), :] = value
        return carry

    lax.fori_loop(0, 32, mask_plane, 0, unroll=4)

    def step(group, carry):
        faces = {}
        for part in range(4):
            x = group * 4 + part
            flag = flags(x)
            new = advance(
                x, lambda i, at: m_ref[tile_rows(i, at), :], gx_ref, gy_ref, gz_ref, flag == 0, row, lane
            )
            c = masked(collide(new), flag)
            for i in range(19):
                out_ref[tile_rows(i, x), :] = c[i]
            join_z_faces(c, x, faces, lane)
        store_z_faces(faces, group, z_ref, 0, lane)
        return carry

    lax.fori_loop(0, 8, step, 0)

    def plane(i, x):
        return out_ref[tile_rows(i, x), :]

    def load_rows(i, q, r):
        return out_ref[pl.ds((i * 32 + q) * 8 + r, 8, stride=32), :]

    y_face = {}
    for face in (2, 3):
        for i in FACE_PDFS[face]:
            y_face[i] = pack_y_face(load_rows, i, face, lane)
    edge_tile = pack_edges(plane, y_face, lane, edge_ref)
    edge_rows = edge_ref[...]
    def put(ref, k, value):
        ref[8 * k : 8 * k + 8, :] = value

    for k in range(5):
        first, second = FACE_PDFS[0][k], FACE_PDFS[1][k]
        put(side_ref, k, jnp.where(there(0), plane(first, 31), plane(second, 0)))
        first, second = FACE_PDFS[2][k], FACE_PDFS[3][k]
        put(side_ref, 5 + k, jnp.where(there(2), y_face[first], y_face[second]))
        put(up_ref, k, z_ref[8 * k : 8 * k + 8, :])
        put(down_ref, k, z_ref[40 + 8 * k : 48 + 8 * k, :])
    put(side_ref, 10, edge_rows)
    put(up_ref, 5, edge_tile)
    put(down_ref, 5, edge_tile)


def last_step_kernel(
    info_ref, in_ref, flag_ref, around_ref, out_hbm, out_ref, gx_ref, gy_ref, gz_ref, sem_ref
):
    row, lane = iotas()

    def there(d):
        return jnp.full((8, 128), info_ref[0, d], jnp.int32) >= 0

    def arrived(d, k):
        place = info_ref[0, d] & 3
        cz = VELOCITY[d + 1][2]
        first = 0 if cz == 0 else (11 if cz < 0 else 17)
        return around_ref[pl.ds(pl.multiple_of(place * 184 + (first + k) * 8, 8), 8), :]

    edge_tile = jnp.zeros((8, 128), jnp.float32)
    for i in range(11, 19):
        edge_tile = jnp.where((lane & 31) == i - 11, arrived(opposite(i) - 1, 5), edge_tile)
    edge_rows = jnp.zeros((8, 128), jnp.float32)
    for i in range(7, 11):
        edge_rows = jnp.where(row == i - 7, arrived(opposite(i) - 1, 10), edge_rows)
    prepare_ghosts(
        lambda face, i: arrived(face ^ 1, FACE_PDFS[face].index(i) + (5 if face in (2, 3) else 0)),
        edge_tile,
        edge_rows,
        there,
        gx_ref,
        gy_ref,
        gz_ref,
        lane,
    )

    def send(group):
        rows = pl.ds(pl.multiple_of(group * 32, 32), 32)
        return pltpu.make_async_copy(out_ref.at[:, rows], out_hbm.at[:, rows], sem_ref.at[group])

    def planes(group, carry):
        for part in range(4):
            x = group * 4 + part
            at = pl.ds(pl.multiple_of(x * 8, 8), 8)
            fluid = flag_ref[at, :] == 0
            new = advance(
                x, lambda i, at: in_ref[tile_rows(i, at), :], gx_ref, gy_ref, gz_ref, fluid, row, lane
            )
            for i in range(19):
                out_ref[i, at, :] = new[i]
        send(group).start()
        return carry

    lax.fori_loop(0, 8, planes, 0)
    for group in range(8):
        send(group).wait()


F32 = jnp.float32
LAYERS = [[4 * k + i for i in range(4)] for k in range(32)]


def scratch(rows, dtype=F32):
    return pltpu.VMEM((rows, 128), dtype)


def array(*shape):
    return jax.ShapeDtypeStruct(shape, F32)


def mebibytes(n):
    return pltpu.CompilerParams(vmem_limit_bytes=n * 1024 * 1024)


def exchange(x):
    return lax.all_to_all(x, "blocks", split_axis=0, concat_axis=0, tiled=True)


def per_device(old_pdfs, old_slot, neighbours, cell_flags):
    flags = cell_flags.reshape(256, 128)
    smem = pl.BlockSpec(memory_space=pltpu.SMEM)
    vmem = pl.BlockSpec(memory_space=pltpu.VMEM)
    rows = old_pdfs.transpose(1, 0, 2).reshape(19, 2, 256, 128)
    rows = rows.transpose(0, 2, 1, 3).reshape(19, 512, 128)

    hbm = pl.BlockSpec(memory_space=pltpu.HBM)
    packed = pl.pallas_call(
        pack_kernel,
        in_specs=[hbm] * 3,
        out_specs=vmem,
        out_shape=array(10240, 128),
        scratch_shapes=[
            pltpu.VMEM((19, 512, 128), F32),
            scratch(160),
            scratch(8),
            pltpu.SMEM((128,), jnp.int32),
            pltpu.SMEM((1, 18), jnp.int32),
            pltpu.SemaphoreType.DMA((10,)),
        ],
        compiler_params=mebibytes(24),
        name="pack",
    )(*(pltpu.with_memory_space_constraint(x, pltpu.HBM) for x in (old_slot, neighbours, rows)))
    spread = exchange(packed.reshape(128, 80, 128))

    picked = pl.pallas_call(
        pick_kernel,
        in_specs=[smem, vmem],
        out_specs=vmem,
        out_shape=array(5120, 128),
        scratch_shapes=[
            scratch(16, jnp.int32),
            pltpu.SMEM((16, 128), jnp.int32),
            pltpu.SemaphoreType.DMA,
        ],
        compiler_params=mebibytes(16),
        name="pick",
    )(old_slot, spread.reshape(10240, 128))
    arrived = exchange(picked.reshape(128, 40, 128))

    ghost_scratch = [scratch(80), scratch(2720), scratch(80)]
    state, side, up, down = pl.pallas_call(
        first_step_kernel,
        in_specs=[smem, vmem, vmem],
        out_specs=[vmem] * 4,
        out_shape=[array(4864, 128), array(88, 128), array(48, 128), array(48, 128)],
        scratch_shapes=[scratch(4864)] + ghost_scratch + [scratch(80), scratch(8)],
        compiler_params=mebibytes(20),
        name="first_step",
    )(neighbours, arrived.reshape(5120, 128), flags)

    below = lax.ppermute(up, "blocks", [(i, i + 4) for i in range(124)])
    above = lax.ppermute(down, "blocks", [(i + 4, i) for i in range(124)])
    around = lax.all_gather(
        jnp.concatenate([side, below, above]), "blocks", axis_index_groups=LAYERS, tiled=True
    )

    new = pl.pallas_call(
        last_step_kernel,
        in_specs=[smem] + [vmem] * 3,
        out_specs=hbm,
        out_shape=array(19, 256, 128),
        scratch_shapes=[pltpu.VMEM((19, 256, 128), F32)]
        + ghost_scratch
        + [pltpu.SemaphoreType.DMA((8,))],
        compiler_params=mebibytes(16),
        name="last_step",
    )(neighbours, state, flags, around)
    return new.reshape(1, 19, 32768)


def solution(mesh):
    in_specs = (P("blocks", None, None), P(), P("blocks", None), P("blocks", None))
    return jax.shard_map(
        per_device,
        mesh=mesh,
        in_specs=in_specs,
        out_specs=P("blocks", None, None),
        check_vma=False,
    )
```

```python
import jax
import jax.numpy as jnp
from jax import lax
from jax.experimental import pallas as pl
from jax.experimental.pallas import tpu as pltpu
from jax.sharding import PartitionSpec as P

EDGE = 32
VELOCITY = (
    (0, 0, 0),
    (1, 0, 0),
    (-1, 0, 0),
    (0, 1, 0),
    (0, -1, 0),
    (0, 0, 1),
    (0, 0, -1),
    (1, 1, 0),
    (-1, -1, 0),
    (1, -1, 0),
    (-1, 1, 0),
    (1, 0, 1),
    (-1, 0, -1),
    (1, 0, -1),
    (-1, 0, 1),
    (0, 1, 1),
    (0, -1, -1),
    (0, 1, -1),
    (0, -1, 1),
)
WEIGHT = (1.0 / 3.0,) + (1.0 / 18.0,) * 6 + (1.0 / 36.0,) * 12
INLET = (0.0, 0.0, 0.05)
WALL = 1e30
OUTLET = 2e30

REST = [3, 4, 5, 6, 7, 8, 9, 10, 11, 12, 13, 14, 15, 16, 17, 18]
POSITION = {0: 7, 1: 11, 2: 15}
POSITION.update(
    zip(REST, [q for q in range(19) if q not in (7, 11, 15)])
)
FACE_PDFS = [
    [i for i in range(19) if VELOCITY[i][axis] == side]
    for axis in range(3)
    for side in (1, -1)
]
Y_PDFS = FACE_PDFS[2] + FACE_PDFS[3]
Z_PDFS = FACE_PDFS[4] + FACE_PDFS[5]
X_PDFS = FACE_PDFS[0] + FACE_PDFS[1]
CARRIERS = [(0, 7), (1, 10), (2, 7), (3, 9), (4, 15), (5, 17)]
TABLE_LANE = 104
EDGE_COLUMNS = [(12, 13), (11, 14), (16, 17), (15, 18)]


def opposite(i):
    return 0 if i == 0 else (i + 1 if i % 2 == 1 else i - 1)


def ghost_places():
    places = {}
    plain = [
        (f, i) for f in range(6) for i in FACE_PDFS[f] if (f, i) not in CARRIERS
    ]
    for n, item in enumerate(plain):
        places[item] = (120 + n // 3, 1 + n % 3)
    for n, item in enumerate(CARRIERS + ["EA", "EB"]):
        places[item] = (120 + n, 4)
    return places


GHOST = ghost_places()
EDGE_CHUNK = GHOST["EA"][0]
TABLE = [(d,) for d in range(6)]
TABLE += [tuple(opposite(i) - 1 for i in pdfs) for pdfs in EDGE_COLUMNS + [(7, 8, 9, 10)]]


def tile_at(i, x):
    pos = POSITION[i]
    chunk = (pos % 4) * 32 + x
    place = pos // 4
    if pos in (7, 11, 15):
        far = x >= 24
        if isinstance(x, int):
            if far:
                return 72 + 8 * ((pos - 7) // 4) + x, 4
            return chunk, place
        chunk = jnp.where(far, 72 + 8 * ((pos - 7) // 4) + x, chunk)
        place = jnp.where(far, 4, place)
    return chunk, place


def inlet_value(i):
    along = sum(c * v for c, v in zip(VELOCITY[i], INLET))
    square = sum(v * v for v in INLET)
    return WEIGHT[i] * (1.0 + 3.0 * along + 4.5 * along * along - 1.5 * square)


def iotas():
    row = lax.broadcasted_iota(jnp.int32, (8, 128), 0)
    lane = lax.broadcasted_iota(jnp.int32, (8, 128), 1)
    return row, lane


def momentum(f):
    jx = (f[1] - f[2]) + (f[7] - f[8]) + (f[9] - f[10]) + (f[11] - f[12]) + (f[13] - f[14])
    jy = (f[3] - f[4]) + (f[7] - f[8]) - (f[9] - f[10]) + (f[15] - f[16]) + (f[17] - f[18])
    jz = (f[5] - f[6]) + (f[11] - f[12]) - (f[13] - f[14]) + (f[15] - f[16]) - (f[17] - f[18])
    return jx, jy, jz


def collide(f):
    even = {i: f[i] + f[i + 1] for i in range(1, 19, 2)}
    odd = {i: f[i] - f[i + 1] for i in range(1, 19, 2)}
    x_xy, y_xy = odd[7] + odd[9], odd[7] - odd[9]
    x_xz, z_xz = odd[11] + odd[13], odd[11] - odd[13]
    y_yz, z_yz = odd[15] + odd[17], odd[15] - odd[17]
    edge_x, edge_y, edge_z = x_xy + x_xz, y_xy + y_yz, z_xz + z_yz
    jx, jy, jz = odd[1] + edge_x, odd[3] + edge_y, odd[5] + edge_z
    flux = [
        edge - 4.0 * axis + (2.0 / 3.0) * j
        for edge, axis, j in ((edge_x, odd[1], jx), (edge_y, odd[3], jy), (edge_z, odd[5], jz))
    ]
    third_x, third_y, third_z = x_xy - x_xz, y_xy - y_yz, z_xz - z_yz
    b_xy, b_xz, b_yz = even[7] + even[9], even[11] + even[13], even[15] + even[17]
    axes = even[1] + even[3] + even[5]
    edges = b_xy + b_xz + b_yz
    density = f[0] + axes + edges
    sx, sy, sz = jx * jx, jy * jy, jz * jz
    square = sx + sy + sz
    energy = -30.0 * f[0] - 11.0 * axes + 8.0 * edges + 11.0 * density - 19.0 * square
    fourth = 12.0 * f[0] - 4.0 * axes + edges - 3.0 * density + 5.5 * square
    rate_e, rate_f = 1.19 / 2394.0, 1.4 / 252.0
    out = [None] * 19
    out[0] = f[0] + (30.0 * rate_e) * energy - (12.0 * rate_f) * fourth
    axis_part = (11.0 * rate_e) * energy + (4.0 * rate_f) * fourth
    edge_part = (-8.0 * rate_e) * energy - rate_f * fourth
    axis_third, edge_third = axes * (1.0 / 3.0), edges * (1.0 / 3.0)
    third_square = square * (1.0 / 3.0)
    axis_delta, edge_delta = [], []
    for a, c, s in ((even[1], b_yz, sx), (even[3], b_xz, sy), (even[5], b_xy, sz)):
        alpha, gamma, tau = a - axis_third, c - edge_third, s - third_square
        p_mode = alpha - gamma - tau
        pi_mode = 0.5 * tau - 2.0 * alpha - gamma
        axis_delta.append(axis_part - (1.6 / 6.0) * p_mode + (2.8 / 12.0) * pi_mode)
        edge_delta.append(edge_part + (1.6 / 6.0) * p_mode + (1.4 / 12.0) * pi_mode)
    for k, i in enumerate((1, 3, 5)):
        odd_part = 0.12 * flux[k]
        out[i] = f[i] + (axis_delta[k] + odd_part)
        out[i + 1] = f[i + 1] + (axis_delta[k] - odd_part)
    fx, fy, fz = (0.03 * v for v in flux)
    hx, hy, hz = 0.2475 * third_x, 0.2475 * third_y, 0.2475 * third_z
    planes = (
        (7, 9, edge_delta[2], jx * jy, fx + hx, fy + hy),
        (11, 13, edge_delta[1], jx * jz, fx - hx, fz + hz),
        (15, 17, edge_delta[0], jy * jz, fy - hy, fz - hz),
    )
    for i, k, delta, cross, first, second in planes:
        shear = 0.4 * (even[i] - even[k] - cross)
        together, against = first + second, first - second
        same, mixed = delta - shear, delta + shear
        out[i] = f[i] + (same - together)
        out[i + 1] = f[i + 1] + (same + together)
        out[k] = f[k] + (mixed - against)
        out[k + 1] = f[k + 1] + (mixed + against)
    return out


def roll_lanes(v, shift):
    if isinstance(shift, int):
        shift = shift % 128
        return v if shift == 0 else pltpu.roll(v, shift, 1)
    return pltpu.roll(v, shift & 127, 1)


def pack_y_face(load_rows, i, face, lane):
    up = face == 2
    packed = None
    for q in range(4):
        rows = load_rows(i, q, 7 if up else 0)
        moved = roll_lanes(rows, 32 * q - 96 if up else 32 * q)
        packed = moved if packed is None else jnp.where((lane >> 5) == q, moved, packed)
    return packed


def join_z_faces(c, x, faces, lane):
    here = (lane & 31) == x
    for n, i in enumerate(Z_PDFS):
        moved = roll_lanes(c[i], x - (31 if n < 5 else 0) + 128)
        faces[n] = jnp.where(here, moved, faces[n]) if n in faces else moved


def store_z_faces(faces, group, z_ref, base, lane):
    here = (lane & 31) >> 2 == group
    for n in range(10):
        rows = slice(base + 8 * n, base + 8 * n + 8)
        z_ref[rows, :] = jnp.where(here, faces[n], z_ref[rows, :])


def pack_edges(plane, y_face, lane, edge_rows_ref):
    tile = jnp.zeros((8, 128), jnp.float32)
    for i in range(11, 19):
        cx, cy, cz = VELOCITY[i]
        source = plane(i, 31 if cx > 0 else 0) if cx else y_face[i]
        moved = roll_lanes(source, i - 11 - (31 if cz > 0 else 0))
        tile = jnp.where((lane & 31) == i - 11, moved, tile)
    edge_rows_ref[...] = jnp.zeros((8, 128), jnp.float32)
    for i in range(7, 11):
        cx, cy, _ = VELOCITY[i]
        line = plane(i, 31 if cx > 0 else 0)
        line = roll_lanes(line, 32 if cy > 0 else 0)
        row = 7 if cy > 0 else 0
        edge_rows_ref[i - 7 : i - 6, :] = line[row : row + 1, :]
    return tile


def pack_kernel(
    old_slot_hbm,
    neighbours_hbm,
    pdf_hbm,
    tiles_ref,
    pdf_ref,
    z_ref,
    edge_ref,
    old_slot_ref,
    neighbours_ref,
    sem_ref,
):
    row, lane = iotas()

    def fetch(g):
        rows = pl.ds(pl.multiple_of(g * 64, 64), 64)
        return pltpu.make_async_copy(pdf_hbm.at[:, rows], pdf_ref.at[:, rows], sem_ref.at[g])

    def fetch_indices():
        return (
            pltpu.make_async_copy(old_slot_hbm, old_slot_ref, sem_ref.at[8]),
            pltpu.make_async_copy(neighbours_hbm, neighbours_ref, sem_ref.at[9]),
        )

    for g in range(8):
        fetch(g).start()
    for copy in fetch_indices():
        copy.start()

    def rows_of(i, x, slot):
        chunk, place = tile_at(i, x)
        return chunk * 80 + slot * 40 + place * 8

    def planes(group, carry):
        fetch(group).wait()
        for slot in range(2):
            faces = {}
            for part in range(4):
                first = pl.multiple_of(group * 64, 64) + part * 16 + slot
                f = [pdf_ref[i, pl.ds(first, 8, stride=2), :] for i in range(19)]
                c = collide(f)
                x = group * 4 + part
                for i in range(19):
                    tiles_ref[pl.ds(pl.multiple_of(rows_of(i, x, slot), 8), 8), :] = c[i]
                join_z_faces(c, x, faces, lane)
            store_z_faces(faces, group, z_ref, 80 * slot, lane)
        return carry

    lax.fori_loop(0, 8, planes, 0)
    for copy in fetch_indices():
        copy.wait()
    table = jnp.zeros((8, 128), jnp.int32)
    for column, directions in enumerate(TABLE):
        other = jnp.int32(0)
        for d in directions:
            other = jnp.maximum(other, neighbours_ref[0, d])
        other = jnp.minimum(other, 127)
        table = jnp.where(lane == TABLE_LANE + column, old_slot_ref[other] * 40, table)
    table = table.astype(jnp.float32)
    free = (row == 7) & (lane >= TABLE_LANE) & (lane < TABLE_LANE + len(TABLE))

    def ghosts(slot, carry):
        def plane(i, x):
            return tiles_ref[pl.ds(pl.multiple_of(rows_of(i, x, slot), 8), 8), :]

        def load_rows(i, q, r):
            return tiles_ref[pl.ds(rows_of(i, q, slot) + r, 8, stride=320), :]

        def put(key, value):
            chunk, place = GHOST[key]
            if place == 4:
                value = jnp.where(free, table, value)
            at = pl.multiple_of(chunk * 80 + slot * 40 + place * 8, 8)
            tiles_ref[pl.ds(at, 8), :] = value

        for face in (0, 1):
            for i in FACE_PDFS[face]:
                put((face, i), plane(i, 31 if face == 0 else 0))
        y_face = {}
        for face in (2, 3):
            for i in FACE_PDFS[face]:
                y_face[i] = pack_y_face(load_rows, i, face, lane)
                put((face, i), y_face[i])
        for n, i in enumerate(Z_PDFS):
            face = 4 + n // 5
            put((face, i), z_ref[pl.ds(pl.multiple_of(80 * slot + 8 * n, 8), 8), :])
        put("EA", pack_edges(plane, y_face, lane, edge_ref))
        put("EB", edge_ref[...])
        return carry

    lax.fori_loop(0, 2, ghosts, 0)


def ghost_code(me, place):
    code = jnp.int32(0)
    for key, (chunk, at) in GHOST.items():
        if at == place and key != "EA":
            code = jnp.where(me == chunk, 10 if key == "EB" else key[0] ^ 1, code)
    return code


def pick_kernel(old_slot_ref, spread_ref, out_ref, table_ref, slots_ref, sem_ref):
    me = lax.axis_index("blocks")
    row, lane = iotas()

    def tile(first, place):
        return spread_ref[pl.ds(pl.multiple_of(first + place * 8, 8), 8), :]

    def store(n, place, value):
        out_ref[pl.ds(pl.multiple_of(n * 40 + place * 8, 8), 8), :] = value

    @pl.when(me < 120)
    def _():
        def own(n, carry):
            slot = old_slot_ref[n] * 40
            for place in range(5):
                store(n, place, tile(slot, place))
            return carry

        lax.fori_loop(0, 128, own, 0, unroll=8)

    @pl.when(me >= 120)
    def _():
        for half in range(2):
            joined = None
            for u in range(8):
                rows = spread_ref[pl.ds((half * 8 + u) * 640 + 39, 8, stride=80), :]
                rows = roll_lanes(rows, 16 * u - TABLE_LANE)
                joined = rows if u == 0 else jnp.where(lane >> 4 == u, rows, joined)
            table_ref[8 * half : 8 * half + 8, :] = joined.astype(jnp.int32)
        copy = pltpu.make_async_copy(table_ref, slots_ref, sem_ref)
        copy.start()


        def own(n, carry):
            store(n, 0, tile(old_slot_ref[n] * 40, 0))
            return carry

        lax.fori_loop(0, 128, own, 0, unroll=16)
        copy.wait()
        codes = [ghost_code(me, place) for place in range(5)]

        def loop(fourth):
            def body(b, carry):
                lane0 = (b & 7) * 16
                for r in range(8):
                    n = b * 8 + r
                    row0 = (b >> 3) * 8 + r
                    for place in range(1, 4):
                        store(n, place, tile(slots_ref[row0, lane0 + codes[place]], place))
                    fourth(n, row0, lane0)
                return carry

            lax.fori_loop(0, 16, body, 0)

        @pl.when(me != EDGE_CHUNK)
        def _():
            loop(lambda n, row0, lane0: store(n, 4, tile(slots_ref[row0, lane0 + codes[4]], 4)))

        @pl.when(me == EDGE_CHUNK)
        def _():
            kind = jnp.zeros((8, 128), jnp.int32)
            for column, pdfs in enumerate(EDGE_COLUMNS):
                for i in pdfs:
                    kind = jnp.where(lane & 31 == i - 11, column, kind)

            def merge(n, row0, lane0):
                value = None
                for column in range(len(EDGE_COLUMNS)):
                    piece = tile(slots_ref[row0, lane0 + 6 + column], 4)
                    value = piece if value is None else jnp.where(kind == column, piece, value)
                store(n, 4, value)

            loop(merge)


def prepare_ghosts(face_tile, edge_tile, edge_rows, there, gx_ref, gy_ref, gz_ref, lane):
    for n, i in enumerate(X_PDFS):
        face = n // 5
        gx_ref[8 * n : 8 * n + 8, :] = jnp.where(there(face ^ 1), face_tile(face, i), WALL)
    for n, i in enumerate(Z_PDFS):
        face = 4 + n // 5
        value = jnp.where(there(face ^ 1), face_tile(face, i), WALL)
        cx = VELOCITY[i][0]
        if cx:
            beyond = -1 if cx > 0 else 32
            line = roll_lanes(edge_tile, beyond - (i - 11))
            line = jnp.where(there(opposite(i) - 1), line, WALL)
            value = jnp.where((lane & 31) == beyond % 32, line, value)
        gz_ref[8 * n : 8 * n + 8, :] = value
    for n, i in enumerate(Y_PDFS):
        face = 2 + n // 5
        cx, cy, cz = VELOCITY[i]
        value = jnp.where(there(face ^ 1), face_tile(face, i), WALL)
        if cz:
            target = 0 if cz > 0 else 31
            line = roll_lanes(edge_tile, target - (i - 11))
            line = jnp.where(there(opposite(i) - 1), line, WALL)
            value = jnp.where((lane & 31) == target, line, roll_lanes(value, cz))
        r = 0 if cy > 0 else 7
        for q in range(4):
            moved = roll_lanes(value, (0 if cy > 0 else 96) - 32 * q)
            gy_ref[pl.ds(272 * n + (q + 1) * 8 + r, 8, stride=32), :] = moved
        if cx:
            line = jnp.where(there(opposite(i) - 1), edge_rows, WALL)
            line = roll_lanes(line, 0 if cy > 0 else 96)
            at = 272 * n + (0 if cx > 0 else 33 * 8) + r
            gy_ref[at : at + 1, :] = line[i - 7 : i - 6, :]


def advance(x, plane, gx_ref, gy_ref, gz_ref, fluid, row, lane):
    own = [plane(i, x) for i in range(19)]
    u = momentum(own)
    base = 1.0 - 1.5 * (u[0] * u[0] + u[1] * u[1] + u[2] * u[2])
    new = [jnp.where(fluid, own[0], 0.0)] + [None] * 18
    low, high = lane < 32, lane >= 96
    first, last = low & (row == 0), high & (row == 7)
    z = (lane & 31)
    for i in range(1, 19):
        cx, cy, cz = VELOCITY[i]
        if cx:
            inside = plane(i, jnp.clip(x - cx, 0, 31))
            n = X_PDFS.index(i)
            border = jnp.full((8, 128), x, jnp.int32) == (0 if cx > 0 else 31)
            source = jnp.where(border, gx_ref[8 * n : 8 * n + 8, :], inside)
        else:
            source = own[i]
        if cz:
            target = 0 if cz > 0 else 31
            n = Z_PDFS.index(i)
            ghost = roll_lanes(gz_ref[8 * n : 8 * n + 8, :], target - (x - cx) + 128)
            source = jnp.where(z == target, ghost, roll_lanes(source, cz))
        if cy:
            n = Y_PDFS.index(i)
            ghost = gy_ref[pl.ds(pl.multiple_of(272 * n + (x - cx + 1) * 8, 8), 8), :]
            turned = roll_lanes(source, 32 * cy)
            carried = pltpu.roll(turned, cy % 8, 0)
            source = jnp.where(low if cy > 0 else high, carried, turned)
            source = jnp.where(first if cy > 0 else last, ghost, source)
        new[i] = source
    for i in range(1, 19, 2):
        cx, cy, cz = VELOCITY[i]
        along = None
        for c, v in zip((cx, cy, cz), u):
            if c:
                along = v * float(c) if along is None else (along + v if c > 0 else along - v)
        even = WEIGHT[i] * (base + 4.5 * along * along)
        odd = (3.0 * WEIGHT[i]) * along
        for k, outlet, bounce in ((i, even + odd, own[i + 1]), (i + 1, even - odd, own[i])):
            value = jnp.where(new[k] < 1.5e30, bounce, outlet)
            value = jnp.where(new[k] < 1e29, new[k], value)
            new[k] = jnp.where(fluid, value, 0.0)
    return new


def masked(c, flag):
    fluid, inlet = flag == 0, flag == 2
    sentinel = jnp.where(flag == 1, WALL, OUTLET)
    return [c[0]] + [
        jnp.where(fluid, c[i], jnp.where(inlet, inlet_value(i), sentinel)) for i in range(1, 19)
    ]


def tile_rows(i, x):
    return pl.ds(pl.multiple_of((i * 32 + x) * 8, 8), 8)


def first_step_kernel(
    info_ref, in_ref, flag_ref, out_ref, side_ref, up_ref, down_ref, m_ref, gx_ref, gy_ref, gz_ref, z_ref, edge_ref
):
    row, lane = iotas()

    def there(d):
        return jnp.full((8, 128), info_ref[0, d], jnp.int32) >= 0

    def arrived(key):
        chunk, place = GHOST[key]
        return in_ref[chunk * 40 + place * 8 : chunk * 40 + place * 8 + 8, :]

    def flags(x):
        return flag_ref[pl.ds(pl.multiple_of(x * 8, 8), 8), :]

    prepare_ghosts(
        lambda face, i: arrived((face, i)),
        arrived("EA"),
        arrived("EB"),
        there,
        gx_ref,
        gy_ref,
        gz_ref,
        lane,
    )

    def mask_plane(x, carry):
        loaded = []
        for i in range(19):
            chunk, place = tile_at(i, x)
            loaded.append(in_ref[pl.ds(pl.multiple_of(chunk * 40 + place * 8, 8), 8), :])
        for i, value in enumerate(masked(loaded, flags(x))):
            m_ref[tile_rows(i, x), :] = value
        return carry

    lax.fori_loop(0, 32, mask_plane, 0, unroll=4)

    def step(group, carry):
        faces = {}
        for part in range(4):
            x = group * 4 + part
            flag = flags(x)
            new = advance(
                x, lambda i, at: m_ref[tile_rows(i, at), :], gx_ref, gy_ref, gz_ref, flag == 0, row, lane
            )
            c = masked(collide(new), flag)
            for i in range(19):
                out_ref[tile_rows(i, x), :] = c[i]
            join_z_faces(c, x, faces, lane)
        store_z_faces(faces, group, z_ref, 0, lane)
        return carry

    lax.fori_loop(0, 8, step, 0)

    def plane(i, x):
        return out_ref[tile_rows(i, x), :]

    def load_rows(i, q, r):
        return out_ref[pl.ds((i * 32 + q) * 8 + r, 8, stride=32), :]

    y_face = {}
    for face in (2, 3):
        for i in FACE_PDFS[face]:
            y_face[i] = pack_y_face(load_rows, i, face, lane)
    edge_tile = pack_edges(plane, y_face, lane, edge_ref)
    edge_rows = edge_ref[...]
    def put(ref, k, value):
        ref[8 * k : 8 * k + 8, :] = value

    for k in range(5):
        first, second = FACE_PDFS[0][k], FACE_PDFS[1][k]
        put(side_ref, k, jnp.where(there(0), plane(first, 31), plane(second, 0)))
        first, second = FACE_PDFS[2][k], FACE_PDFS[3][k]
        put(side_ref, 5 + k, jnp.where(there(2), y_face[first], y_face[second]))
        put(up_ref, k, z_ref[8 * k : 8 * k + 8, :])
        put(down_ref, k, z_ref[40 + 8 * k : 48 + 8 * k, :])
    put(side_ref, 10, edge_rows)
    put(up_ref, 5, edge_tile)
    put(down_ref, 5, edge_tile)


def last_step_kernel(
    info_ref, in_ref, flag_ref, around_ref, out_hbm, out_ref, gx_ref, gy_ref, gz_ref, sem_ref
):
    row, lane = iotas()

    def there(d):
        return jnp.full((8, 128), info_ref[0, d], jnp.int32) >= 0

    def arrived(d, k):
        place = info_ref[0, d] & 3
        cz = VELOCITY[d + 1][2]
        first = 0 if cz == 0 else (11 if cz < 0 else 17)
        return around_ref[pl.ds(pl.multiple_of(place * 184 + (first + k) * 8, 8), 8), :]

    edge_tile = jnp.zeros((8, 128), jnp.float32)
    for i in range(11, 19):
        edge_tile = jnp.where((lane & 31) == i - 11, arrived(opposite(i) - 1, 5), edge_tile)
    edge_rows = jnp.zeros((8, 128), jnp.float32)
    for i in range(7, 11):
        edge_rows = jnp.where(row == i - 7, arrived(opposite(i) - 1, 10), edge_rows)
    prepare_ghosts(
        lambda face, i: arrived(face ^ 1, FACE_PDFS[face].index(i) + (5 if face in (2, 3) else 0)),
        edge_tile,
        edge_rows,
        there,
        gx_ref,
        gy_ref,
        gz_ref,
        lane,
    )

    def send(group):
        rows = pl.ds(pl.multiple_of(group * 32, 32), 32)
        return pltpu.make_async_copy(out_ref.at[:, rows], out_hbm.at[:, rows], sem_ref.at[group])

    def planes(group, carry):
        for part in range(4):
            x = group * 4 + part
            at = pl.ds(pl.multiple_of(x * 8, 8), 8)
            fluid = flag_ref[at, :] == 0
            new = advance(
                x, lambda i, at: in_ref[tile_rows(i, at), :], gx_ref, gy_ref, gz_ref, fluid, row, lane
            )
            for i in range(19):
                out_ref[i, at, :] = new[i]
        send(group).start()
        return carry

    lax.fori_loop(0, 8, planes, 0)
    for group in range(8):
        send(group).wait()


F32 = jnp.float32
LAYERS = [[4 * k + i for i in range(4)] for k in range(32)]


def scratch(rows, dtype=F32):
    return pltpu.VMEM((rows, 128), dtype)


def array(*shape):
    return jax.ShapeDtypeStruct(shape, F32)


def mebibytes(n):
    return pltpu.CompilerParams(vmem_limit_bytes=n * 1024 * 1024)


def exchange(x):
    return lax.all_to_all(x, "blocks", split_axis=0, concat_axis=0, tiled=True)


def per_device(old_pdfs, old_slot, neighbours, cell_flags):
    flags = cell_flags.reshape(256, 128)
    smem = pl.BlockSpec(memory_space=pltpu.SMEM)
    vmem = pl.BlockSpec(memory_space=pltpu.VMEM)
    rows = old_pdfs.transpose(1, 0, 2).reshape(19, 2, 256, 128)
    rows = rows.transpose(0, 2, 1, 3).reshape(19, 512, 128)

    hbm = pl.BlockSpec(memory_space=pltpu.HBM)
    packed = pl.pallas_call(
        pack_kernel,
        in_specs=[hbm] * 3,
        out_specs=vmem,
        out_shape=array(10240, 128),
        scratch_shapes=[
            pltpu.VMEM((19, 512, 128), F32),
            scratch(160),
            scratch(8),
            pltpu.SMEM((128,), jnp.int32),
            pltpu.SMEM((1, 18), jnp.int32),
            pltpu.SemaphoreType.DMA((10,)),
        ],
        compiler_params=mebibytes(24),
        name="pack",
    )(*(pltpu.with_memory_space_constraint(x, pltpu.HBM) for x in (old_slot, neighbours, rows)))
    spread = exchange(packed.reshape(128, 80, 128))

    picked = pl.pallas_call(
        pick_kernel,
        in_specs=[smem, vmem],
        out_specs=vmem,
        out_shape=array(5120, 128),
        scratch_shapes=[
            scratch(16, jnp.int32),
            pltpu.SMEM((16, 128), jnp.int32),
            pltpu.SemaphoreType.DMA,
        ],
        compiler_params=mebibytes(16),
        name="pick",
    )(old_slot, spread.reshape(10240, 128))
    arrived = exchange(picked.reshape(128, 40, 128))

    ghost_scratch = [scratch(80), scratch(2720), scratch(80)]
    state, side, up, down = pl.pallas_call(
        first_step_kernel,
        in_specs=[smem, vmem, vmem],
        out_specs=[vmem] * 4,
        out_shape=[array(4864, 128), array(88, 128), array(48, 128), array(48, 128)],
        scratch_shapes=[scratch(4864)] + ghost_scratch + [scratch(80), scratch(8)],
        compiler_params=mebibytes(20),
        name="first_step",
    )(neighbours, arrived.reshape(5120, 128), flags)

    below = lax.ppermute(up, "blocks", [(i, i + 4) for i in range(124)])
    above = lax.ppermute(down, "blocks", [(i + 4, i) for i in range(124)])
    around = lax.all_gather(
        jnp.concatenate([side, below, above]), "blocks", axis_index_groups=LAYERS, tiled=True
    )

    new = pl.pallas_call(
        last_step_kernel,
        in_specs=[smem] + [vmem] * 3,
        out_specs=hbm,
        out_shape=array(19, 256, 128),
        scratch_shapes=[pltpu.VMEM((19, 256, 128), F32)]
        + ghost_scratch
        + [pltpu.SemaphoreType.DMA((8,))],
        compiler_params=mebibytes(16),
        name="last_step",
    )(neighbours, state, flags, around)
    return new.reshape(1, 19, 32768)


def solution(mesh):
    in_specs = (P("blocks", None, None), P(), P("blocks", None), P("blocks", None))
    return jax.shard_map(
        per_device,
        mesh=mesh,
        in_specs=in_specs,
        out_specs=P("blocks", None, None),
        check_vma=False,
    )
```
